512 devices in a mesh: req: 256 (over z, y, x), head: 2 (over core).
Axes of the slice: x: 4, y: 8, z: 8, core: 2. Of those that a mesh axis runs over, the one named last changes fastest.
Arguments:
- hidden_in: bfloat16 [12288, 1536], P('req', 'head'), may hold values from -6 to 6
- norm_gain: float32 [1536], replicated, may hold values from 0.5 to 1.5
- proj_gate: bfloat16 [1536, 3072], P(None, 'head'), may hold values from -0.15625 to 0.15625
- proj_inner: bfloat16 [1536, 3072], P(None, 'head'), may hold values from -0.15625 to 0.15625
- proj_ssm: bfloat16 [1536, 256], P(None, 'head'), may hold values from -0.15625 to 0.15625
- proj_step: bfloat16 [1536, 48], P(None, 'head'), may hold values from -0.15625 to 0.15625
- step_bias: float32 [48], P('head'), may hold values from -6 to -1
- decay_log: float32 [48], P('head'), may hold values from 0 to 2.77
- skip_gain: float32 [48], P('head'), may hold values from 0.5 to 1.5
- conv_inner: bfloat16 [4, 3072], P(None, 'head'), may hold values from -3 to 3
- conv_inner_bias: float32 [3072], P('head'), may hold values from -3 to 3
- conv_ssm: bfloat16 [4, 256], replicated, may hold values from -3 to 3
- conv_ssm_bias: float32 [256], replicated, may hold values from -3 to 3
- gate_gain: float32 [3072], P('head'), may hold values from 0.5 to 1.5
- proj_out: bfloat16 [3072, 1536], P('head'), may hold values from -0.109375 to 0.109375
- states_in: bfloat16 [1536, 48, 64, 128], P('req', 'head'), may hold values from -6 to 6
- edge_inner: bfloat16 [1536, 3, 3072], P('req', None, 'head'), may hold values from -6 to 6
- edge_ssm: bfloat16 [1536, 3, 256], P('req'), may hold values from -6 to 6
- draft_lengths: int32 [1536], P('req'), may hold values from 1 to 8, as said below
- accepted: int32 [1536], P('req'), may hold values from 0 to 8, as said below
- destination: int32 [1536], P('req'), may hold values from 0 to 1535, as said below
Outputs:
- hidden_out: bfloat16 [12288, 1536], P('req', 'head')
- kept_state: bfloat16 [1536, 48, 64, 128], P('req', 'head')
- kept_edge_inner: bfloat16 [1536, 3, 3072], P('req', None, 'head')
- kept_edge_ssm: bfloat16 [1536, 3, 256], P('req')
The draws below stay inside these ranges and needn't reach their ends.
Inputs may be any that keep to these rules, and one draw needn't show every extreme that they name: `draft_lengths`: in every draw some request has a draft of 8 tokens. accepted[r] <= draft_lengths[r]; in every draw some request accepts none and some accepts 8. `destination`: a permutation of the 1536 output rows; row d lies on index d // 6 of req; a request on index i of req goes to index (i + k) mod 256 for some k of 0 .. 7; the 6 requests of one index use 6 different k, the same set of k on every index, so every index receives exactly one request from each of 6 senders.
All inputs are finite; a program needn't handle non-finite values.
Results may differ from the reference program's by a relative error of at most 0.015.
Values may be sent and summed in bfloat16 or wider, within the bound.
A program may use at most 128 MiB of HBM per device.

```python
import jax
import jax.numpy as jnp
from jax import lax

D = 1536
HEADS = 48
HEAD_DIM = 64
NSTATE = 128
KCONV = 4
DRAFT = 8
WINDOW = 8
REQ_DEV = 6
DINNER = 3072
REQUESTS = 1536
TOKENS = 12288
N_REQ = 256


def draft_plan(key):
    base = jax.random.fold_in(key, 11)
    first, second, third, fourth = jax.random.split(base, 4)
    ceilings = jax.random.randint(first, (N_REQ, 1), 1, DRAFT + 1)
    raw_lengths = jax.random.randint(second, (N_REQ, REQ_DEV), 0, 1 << 20)
    lengths_all = (1 + raw_lengths % ceilings).reshape(-1)
    chosen = jax.random.randint(third, (), 0, REQUESTS)
    other = (chosen + 1) % REQUESTS
    rows = jnp.arange(REQUESTS, dtype=jnp.int32)
    lengths_all = jnp.where(rows == chosen, DRAFT, lengths_all)
    raw_accept = jax.random.randint(fourth, (REQUESTS,), 0, 1 << 20)
    accept_all = raw_accept % (lengths_all + 1)
    accept_all = jnp.where(rows == chosen, DRAFT, accept_all)
    accept_all = jnp.where(rows == other, 0, accept_all)
    return (lengths_all.astype(jnp.int32), accept_all.astype(jnp.int32))


def draw_draft_lengths(key, part):
    return draft_plan(key)[0]


def draw_accepted(key, part):
    return draft_plan(key)[1]


def draw_destination(key, part):
    base = jax.random.fold_in(key, 23)
    first, second = jax.random.split(base, 2)
    offsets = jax.random.permutation(first, WINDOW)[:REQ_DEV].astype(jnp.int32)
    order = jax.random.permutation(second, REQ_DEV).astype(jnp.int32)
    senders = jnp.arange(N_REQ, dtype=jnp.int32)[:, None]
    owners = (senders + offsets[None, :]) % N_REQ
    slots = (order[None, :] + owners) % REQ_DEV
    return (owners * REQ_DEV + slots).reshape(-1).astype(jnp.int32)


def steps_of(rng, extent, cuts, low, high):
    def one(dim, blocks):
        steps = jax.random.uniform(jax.random.fold_in(jax.random.fold_in(rng, 6), dim), (blocks,), jnp.float32, low / len(cuts), high / len(cuts))
        return jnp.repeat(jnp.exp(steps), extent[dim] // blocks).reshape((-1,) + (1,) * (len(extent) - dim - 1))

    level = one(*cuts[0])
    for cut in cuts[1:]:
        level = level * one(*cut)
    return level


def normal_values(key, dims, scale, limit, pieces=(), kind=jnp.bfloat16):
    drawn = jax.random.normal(key, dims, jnp.float32) * scale
    if len(pieces) > 0:
        drawn = steps_of(key, dims, pieces, -0.22, 0.18) * drawn
    return jnp.clip(drawn, min=-limit, max=limit).astype(kind)


def setup_inputs(seed: int = 0) -> dict:
    seeds = jax.random.split(jax.random.key(seed), 22)
    hidden_in = normal_values(seeds[0], (TOKENS, D), 1.0, 6.0, ((0, 256), (1, 2)))
    norm_gain = jnp.clip(1.0 + 0.1 * jax.random.normal(seeds[1], (D,), jnp.float32), 0.5, 1.5)
    proj_gate = normal_values(seeds[2], (D, DINNER), D ** -0.5, 0.15625, ((1, 2),))
    proj_inner = normal_values(seeds[3], (D, DINNER), D ** -0.5, 0.15625, ((1, 2),))
    proj_ssm = normal_values(seeds[4], (D, 2 * NSTATE), D ** -0.5, 0.15625, ((1, 2),))
    proj_step = normal_values(seeds[5], (D, HEADS), D ** -0.5, 0.15625, ((1, 2),))
    step_bias = jnp.clip(-6.0 + 5.0 * jax.random.uniform(seeds[6], (HEADS,), jnp.float32) ** steps_of(seeds[6], (HEADS,), ((0, 2),), -0.2, 0.2), -6.0, -1.0)
    decay_log = jnp.clip(2.77 * jax.random.uniform(seeds[7], (HEADS,), jnp.float32) ** steps_of(seeds[7], (HEADS,), ((0, 2),), -0.2, 0.2), 0.0, 2.77)
    skip_gain = jnp.clip(0.5 + 1.0 * jax.random.uniform(seeds[8], (HEADS,), jnp.float32) ** steps_of(seeds[8], (HEADS,), ((0, 2),), -0.2, 0.2), 0.5, 1.5)
    conv_inner = normal_values(seeds[9], (KCONV, DINNER), KCONV ** -0.5, 3.0, ((1, 2),))
    conv_inner_bias = normal_values(seeds[10], (DINNER,), 0.5, 3.0, ((0, 2),), jnp.float32)
    conv_ssm = normal_values(seeds[11], (KCONV, 2 * NSTATE), KCONV ** -0.5, 3.0)
    conv_ssm_bias = normal_values(seeds[12], (2 * NSTATE,), 0.5, 3.0, (), jnp.float32)
    gate_gain = jnp.clip(1.0 + 0.1 * jax.random.normal(seeds[13], (DINNER,), jnp.float32), 0.5, 1.5)
    proj_out = normal_values(seeds[14], (DINNER, D), DINNER ** -0.5, 0.109375, ((0, 2),))
    states_in = normal_values(seeds[15], (REQUESTS, HEADS, HEAD_DIM, NSTATE), 1.0, 6.0, ((0, 256), (1, 2)))
    edge_inner = normal_values(seeds[16], (REQUESTS, KCONV - 1, DINNER), 1.0, 6.0, ((0, 256), (2, 2)))
    edge_ssm = normal_values(seeds[17], (REQUESTS, KCONV - 1, 2 * NSTATE), 1.0, 6.0, ((0, 256),))
    draft_lengths = draw_draft_lengths(jax.random.fold_in(seeds[21], 71), 0)
    accepted = draw_accepted(jax.random.fold_in(seeds[21], 71), 0)
    destination = draw_destination(jax.random.fold_in(seeds[21], 71), 0)
    return dict(hidden_in=hidden_in, norm_gain=norm_gain, proj_gate=proj_gate, proj_inner=proj_inner, proj_ssm=proj_ssm, proj_step=proj_step, step_bias=step_bias, decay_log=decay_log, skip_gain=skip_gain, conv_inner=conv_inner, conv_inner_bias=conv_inner_bias, conv_ssm=conv_ssm, conv_ssm_bias=conv_ssm_bias, gate_gain=gate_gain, proj_out=proj_out, states_in=states_in, edge_inner=edge_inner, edge_ssm=edge_ssm, draft_lengths=draft_lengths, accepted=accepted, destination=destination)


epsilon = 1e-05

def causal_conv(edge, rows, weight, bias):
    full = jnp.concatenate([edge, rows], axis=1)
    total = jnp.zeros(rows.shape, jnp.float32) + bias.astype(jnp.float32)
    for offset in range(KCONV):
        total = total + full[:, offset:offset + DRAFT, :].astype(jnp.float32) * weight[offset].astype(jnp.float32)
    return (jax.nn.silu(total).astype(jnp.bfloat16), full)

def edge_rows(full, accepted):
    index = accepted[:, None] + jnp.arange(KCONV - 1, dtype=jnp.int32)[None, :]
    return jnp.take_along_axis(full, index[:, :, None].astype(jnp.int32), axis=1)

def advance(state, kept, step_now, inner_now, bmat, cmat, rates, skip_gain, accepted, position):
    state = jnp.exp(step_now * rates)[:, :, None, None] * state + (step_now[:, :, None] * inner_now)[:, :, :, None] * bmat[:, None, None, :]
    output = jnp.einsum('rhpn,rn->rhp', state, cmat, precision=lax.Precision.HIGHEST) + skip_gain[None, :, None] * inner_now
    kept = jnp.where((accepted == position + 1)[:, None, None, None], state, kept)
    return (state, kept, output)

def reference(hidden_in, norm_gain, proj_gate, proj_inner, proj_ssm, proj_step, step_bias, decay_log, skip_gain, conv_inner, conv_inner_bias, conv_ssm, conv_ssm_bias, gate_gain, proj_out, states_in, edge_inner, edge_ssm, draft_lengths, accepted, destination):
    wide = hidden_in.astype(jnp.float32)
    normed = (wide * lax.rsqrt(lax.optimization_barrier(jnp.mean(wide * wide, axis=-1, keepdims=True)) + epsilon) * norm_gain).astype(jnp.bfloat16)
    gate = jnp.dot(normed, proj_gate, preferred_element_type=jnp.float32).astype(jnp.bfloat16)
    inner = jnp.dot(normed, proj_inner, preferred_element_type=jnp.float32).astype(jnp.bfloat16)
    ssm_rows = jnp.dot(normed, proj_ssm, preferred_element_type=jnp.float32).astype(jnp.bfloat16)
    step_raw = jnp.dot(normed, proj_step, preferred_element_type=jnp.float32).astype(jnp.bfloat16)
    conv_x, full_inner = causal_conv(edge_inner, inner.reshape(REQUESTS, DRAFT, DINNER), conv_inner, conv_inner_bias)
    conv_s, full_ssm = causal_conv(edge_ssm, ssm_rows.reshape(REQUESTS, DRAFT, 2 * NSTATE), conv_ssm, conv_ssm_bias)
    live = (jnp.arange(DRAFT, dtype=jnp.int32)[None, :] < draft_lengths[:, None]).astype(jnp.float32)
    step_size = jax.nn.softplus(step_raw.astype(jnp.float32).reshape(REQUESTS, DRAFT, HEADS) + step_bias) * live[:, :, None]
    rates = -jnp.exp(decay_log)

    def one_block(block):
        start_state, inner_block, ssm_block, step_block, accepted_block = block
        state = start_state.astype(jnp.float32)
        kept = jnp.where((accepted_block == 0)[:, None, None, None], state, jnp.zeros_like(state))
        outputs = []
        for position in range(DRAFT):
            state, kept, output = advance(state, kept, step_block[:, position], inner_block[:, position].astype(jnp.float32), ssm_block[:, position, :NSTATE].astype(jnp.float32), ssm_block[:, position, NSTATE:].astype(jnp.float32), rates, skip_gain, accepted_block, position)
            outputs.append(output)
        return (jnp.stack(outputs, axis=1).astype(jnp.bfloat16), kept.astype(jnp.bfloat16))
    blocks = (states_in.reshape(N_REQ, REQ_DEV, HEADS, HEAD_DIM, NSTATE), conv_x.reshape(N_REQ, REQ_DEV, DRAFT, HEADS, HEAD_DIM), conv_s.reshape(N_REQ, REQ_DEV, DRAFT, 2 * NSTATE), step_size.reshape(N_REQ, REQ_DEV, DRAFT, HEADS), accepted.reshape(N_REQ, REQ_DEV))
    ssm_out, kept = lax.map(one_block, blocks)
    ssm_out = ssm_out.reshape(TOKENS, DINNER)
    kept = kept.reshape(REQUESTS, HEADS, HEAD_DIM, NSTATE)
    gated = ssm_out.astype(jnp.float32) * jax.nn.silu(gate.astype(jnp.float32))
    gated_norm = (gated * lax.rsqrt(lax.optimization_barrier(jnp.mean(gated * gated, axis=-1, keepdims=True)) + epsilon) * gate_gain).astype(jnp.bfloat16)
    mixed = jnp.dot(gated_norm, proj_out, preferred_element_type=jnp.float32)
    hidden_out = (wide + mixed).astype(jnp.bfloat16)
    kept_state = jnp.zeros_like(kept).at[destination].set(kept)
    kept_edge_inner = jnp.zeros_like(edge_inner).at[destination].set(edge_rows(full_inner, accepted))
    kept_edge_ssm = jnp.zeros_like(edge_ssm).at[destination].set(edge_rows(full_ssm, accepted))
    return (hidden_out, kept_state, kept_edge_inner, kept_edge_ssm)
```

```python
import functools

import jax
import jax.numpy as jnp
from jax import lax
from jax.experimental import pallas as pl
from jax.experimental.pallas import tpu as pltpu
from jax.sharding import PartitionSpec as P

HEAD_DIM = 64
NSTATE = 128
KCONV = 4
DRAFT = 8
WINDOW = 8
DINNER = 3072
EPS = 1e-05
MESH = pl.DeviceIdType.MESH
F32 = jnp.float32
BF16 = jnp.bfloat16
PACK_ROWS = 16


def silu(value):
    return value * jax.nn.sigmoid(value)


def finish_rows(state, factors, bmat):
    row = lax.broadcasted_iota(jnp.int32, (PACK_ROWS, NSTATE), 0)
    decay = jnp.where((row == 8) | (row == 9), 1.0, 0.0).astype(BF16)
    padded = jnp.concatenate([bmat, jnp.zeros_like(bmat)], axis=0)
    right = jnp.concatenate([padded, decay], axis=1)
    both = lax.dot_general(factors, right, (((0,), (0,)), ((), ())), preferred_element_type=F32)
    return (state.astype(F32) * both[:, NSTATE:] + both[:, :NSTATE]).astype(BF16)


def layer_kernel(
    sizes,
    lengths,
    accepted,
    destination,
    hid,
    norm_gain,
    step_bias,
    decay_log,
    skip_gain,
    conv_i,
    bias_i,
    conv_s,
    bias_s,
    gate_gain,
    edge_i,
    edge_s,
    wg_hbm,
    wi_hbm,
    ws_hbm,
    wt_hbm,
    wo_hbm,
    st_hbm,
    got_state,
    got_pack,
    hidden_out,
    wg,
    wi,
    ws,
    wt,
    wo,
    st,
    send,
    packs,
    pack_f,
    whole,
    nrm,
    seq_i,
    seq_s,
    ssm_own,
    ssm_got,
    gate,
    steps,
    vec,
    vec_x,
    gated,
    sq_own,
    sq_got,
    part,
    part_got,
    local_sem,
    send_sem,
    recv_sem,
):
    peers, count, heads = sizes
    rows = count * DRAFT
    half = hid.shape[1]
    width = wg.shape[1]
    me = lax.axis_index("req")
    head = lax.axis_index("head")
    other = 1 - head

    local = []
    for i, (src, dst) in enumerate(
        (
            (st_hbm, st),
            (ws_hbm, ws),
            (wt_hbm, wt),
            (wi_hbm, wi),
            (wg_hbm, wg),
            (wo_hbm, wo),
        )
    ):
        copy = pltpu.make_async_copy(src, dst, local_sem.at[i])
        copy.start()
        local.append(copy)

    def at(offset):
        return {"req": lax.rem(me + offset + peers, peers), "head": head}

    partner = {"req": me, "head": other}
    barrier = pltpu.get_barrier_semaphore()
    for k in range(1, WINDOW):
        pl.semaphore_signal(barrier, inc=1, device_id=at(k), device_id_type=MESH)
        pl.semaphore_signal(barrier, inc=1, device_id=at(-k), device_id_type=MESH)
    pl.semaphore_signal(barrier, inc=1, device_id=partner, device_id_type=MESH)
    pl.semaphore_wait(barrier, 2 * WINDOW - 1)

    def remote(src, dst, i, device):
        return pltpu.make_async_remote_copy(
            src_ref=src,
            dst_ref=dst,
            send_sem=send_sem.at[i],
            recv_sem=recv_sem.at[i],
            device_id=device,
            device_id_type=MESH,
        )

    to_partner = remote(hid, whole.at[head], 0, partner)
    to_partner.start()

    reach, slots = [], []
    for r in range(count):
        target = destination[r]
        owner = lax.div(target, count)
        reach.append(lax.rem(owner - me + peers, peers))
        slots.append(target - owner * count)
    picks, valid = [], []
    for k in range(WINDOW):
        pick = jnp.int32(0)
        found = jnp.int32(0)
        for r in range(count):
            hit = reach[r] == k
            pick = jnp.where(hit, jnp.int32(r), pick)
            found = jnp.where(hit, jnp.int32(1), found)
        picks.append(pick)
        valid.append(found)

    local[0].wait()
    moves = []
    for k in range(WINDOW - 1, 0, -1):
        send[k] = st[picks[k]]
        copy = remote(send.at[k], got_state.at[k], k, at(k))
        copy.start()
        moves.append(copy)
    send[0] = st[picks[0]]
    own_state = pltpu.make_async_copy(send.at[0], got_state.at[0], local_sem.at[6])
    own_state.start()

    whole[pl.ds(head, 1)] = hid[...][None]
    to_partner.wait()
    left = whole[0].astype(F32)
    right = whole[1].astype(F32)
    mean = (
        jnp.sum(left * left, axis=-1, keepdims=True) + jnp.sum(right * right, axis=-1, keepdims=True)
    ) / (2 * half)
    scale = lax.rsqrt(mean + EPS)
    nrm[:, :half] = (left * scale * norm_gain[:, :half]).astype(BF16)
    nrm[:, half:] = (right * scale * norm_gain[:, half:]).astype(BF16)

    local[1].wait()
    ssm_own[...] = jnp.dot(nrm[...], ws[...], preferred_element_type=F32).astype(BF16)
    ssm_move = remote(ssm_own, ssm_got, 8, partner)
    ssm_move.start()

    spread = (
        lax.shift_right_logical(lax.broadcasted_iota(jnp.int32, (heads, width), 1), 6)
        == lax.broadcasted_iota(jnp.int32, (heads, width), 0)
    ).astype(F32)
    vec[...] = jnp.zeros_like(vec)
    vec[0:1, :] = step_bias[...]
    vec[1:2, :] = decay_log[...]
    vec[2:3, :] = skip_gain[...]
    vec_x[...] = jnp.dot(
        vec[...], spread, precision=lax.Precision.HIGHEST, preferred_element_type=F32
    )
    local[2].wait()
    step_raw = jnp.dot(nrm[...], wt[...], preferred_element_type=F32).astype(BF16)
    step_x = jnp.dot(step_raw, spread.astype(BF16), preferred_element_type=F32) + vec_x[0:1, :]
    steps[...] = jnp.maximum(step_x, 0.0) + jnp.log1p(jnp.exp(-jnp.abs(step_x)))

    tile = 256
    local[3].wait()

    def project_inner(j, carry):
        cols = pl.ds(pl.multiple_of(j * tile, tile), tile)
        value = jnp.dot(nrm[...], wi[:, cols], preferred_element_type=F32)
        value = value.astype(BF16).astype(F32)
        for r in range(count):
            seq_i[r, 8:16, cols] = value[r * DRAFT : (r + 1) * DRAFT]
        return carry

    lax.fori_loop(0, width // tile, project_inner, 0)
    local[4].wait()

    def project_gate(j, carry):
        cols = pl.ds(pl.multiple_of(j * tile, tile), tile)
        value = jnp.dot(nrm[...], wg[:, cols], preferred_element_type=F32)
        value = value.astype(BF16).astype(F32)
        gate[:, cols] = silu(value)
        return carry

    lax.fori_loop(0, width // tile, project_gate, 0)

    ssm_move.wait()
    own_cols = ssm_own[...].astype(F32)
    got_cols = ssm_got[...].astype(F32)
    first = head == 0
    bcols = jnp.where(first, own_cols, got_cols)
    ccols = jnp.where(first, got_cols, own_cols)
    for r in range(count):
        seq_i[r, 5:8, :] = edge_i[r].astype(F32)
        seq_s[r, 5:8, :] = edge_s[r].astype(F32)
        seq_s[r, 8:16, :NSTATE] = bcols[r * DRAFT : (r + 1) * DRAFT]
        seq_s[r, 8:16, NSTATE:] = ccols[r * DRAFT : (r + 1) * DRAFT]

    slot_of = slots

    def one_request(r, carry):
        block = pl.ds(pl.multiple_of(r * DRAFT, DRAFT), DRAFT)
        total = jnp.zeros((DRAFT, width), F32) + bias_i[...]
        narrow = jnp.zeros((DRAFT, 2 * NSTATE), F32) + bias_s[...]
        for k in range(KCONV):
            total = total + seq_i[r, 5 + k : 13 + k, :] * conv_i[k : k + 1, :].astype(F32)
            narrow = narrow + seq_s[r, 5 + k : 13 + k, :] * conv_s[k : k + 1, :].astype(F32)
        x = silu(total).astype(BF16).astype(F32)
        bc = silu(narrow).astype(BF16)
        bmat, cmat = bc[:, :NSTATE], bc[:, NSTATE:]
        when = lax.broadcasted_iota(jnp.int32, (DRAFT, width), 0)
        step = jnp.where(when < lengths[r], steps[block, :], 0.0)
        change = step * -jnp.exp(vec_x[1:2, :])
        decay = change
        for shift in (1, 2, 4):
            decay = decay + jnp.where(when >= shift, pltpu.roll(decay, shift, 0), 0.0)
        weighted = step * x
        pair = lax.dot_general(cmat, bmat, (((1,), (1,)), ((), ())), preferred_element_type=F32)
        seen = lax.dot_general(cmat, st[r], (((1,), (1,)), ((), ())), preferred_element_type=F32)
        out = jnp.exp(decay) * seen + vec_x[2:3, :] * x
        for u in range(DRAFT):
            lag = jnp.where(when >= u, decay - decay[u : u + 1, :], -1e30)
            out = out + jnp.exp(lag) * pair[:, u : u + 1] * weighted[u : u + 1, :]
        ssm_out = out.astype(BF16).astype(F32)
        value = ssm_out * gate[block, :]
        gated[block, :] = value
        sq_own[block, :] = jnp.broadcast_to(
            jnp.sum(value * value, axis=-1, keepdims=True), (DRAFT, NSTATE)
        )
        taken = accepted[r]
        end = jnp.sum(jnp.where(when < taken, change, 0.0), axis=0, keepdims=True)
        lag = jnp.where(when < taken, end - decay, -1e30)
        pack_f[r, 0:8, :width] = jnp.exp(lag) * weighted
        whole_decay = jnp.exp(end)
        high = whole_decay.astype(BF16).astype(F32)
        pack_f[r, 8:9, :width] = high
        pack_f[r, 9:10, :width] = whole_decay - high
        for i in range(KCONV - 1):
            pack_f[r, 10 + i : 11 + i, :width] = seq_i[r, pl.ds(5 + taken + i, 1), :]
            pack_f[r, 8 + i : 9 + i, width:] = seq_s[r, pl.ds(5 + taken + i, 1), :]
        pack_f[r, 0:8, width : width + NSTATE] = bmat.astype(F32)
        pack_f[r, 0:8, width + NSTATE :] = jnp.zeros((8, NSTATE), F32)
        slot = slot_of[0]
        for q in range(1, count):
            slot = jnp.where(r == q, slot_of[q], slot)
        pack_f[r, 13:16, :width] = jnp.zeros((3, width), F32)
        pack_f[r, 11:16, width:] = jnp.zeros((5, 2 * NSTATE), F32) + slot.astype(F32)
        return carry

    lax.fori_loop(0, count, one_request, 0)

    sq_move = remote(sq_own, sq_got, 9, partner)
    sq_move.start()
    for k in range(WINDOW - 1, 0, -1):
        packs[k] = jnp.where(valid[k] > 0, pack_f[picks[k]], -1.0).astype(BF16)
        copy = remote(packs.at[k], got_pack.at[k], 10 + k, at(k))
        copy.start()
        moves.append(copy)
    packs[0] = jnp.where(valid[0] > 0, pack_f[picks[0]], -1.0).astype(BF16)
    own_pack = pltpu.make_async_copy(packs.at[0], got_pack.at[0], local_sem.at[7])
    own_pack.start()

    sq_move.wait()
    square = (sq_own[:, 0:1] + sq_got[:, 0:1]) / DINNER
    nrm[...] = (gated[...] * lax.rsqrt(square + EPS) * gate_gain[...]).astype(BF16)

    local[5].wait()
    per = half // tile

    def project_out(j, carry):
        which = jnp.where(j < per, other, head)
        i = jnp.where(j < per, j, j - per)
        cols = pl.ds(pl.multiple_of(which * half + i * tile, tile), tile)
        value = jnp.dot(nrm[...], wo[:, cols], preferred_element_type=F32)
        part[pl.ds(jnp.where(j < per, 0, 1), 1), :, pl.ds(pl.multiple_of(i * tile, tile), tile)] = value[None]
        return carry

    lax.fori_loop(0, per, project_out, 0)
    part_move = remote(part.at[0], part_got, 18, partner)
    part_move.start()
    lax.fori_loop(per, 2 * per, project_out, 0)
    part_move.wait()
    hidden_out[...] = (hid[...].astype(F32) + part[1] + part_got[...]).astype(BF16)

    own_state.wait()
    own_pack.wait()
    for copy in moves:
        copy.wait()


def place_kernel(
    sizes, got_state, got_pack, hidden, kept, kept_i, kept_s, hidden_out, sin, pin, sout, iout, eout, in_sem, out_sem
):
    count, width = sizes
    loads = []
    for k in range(WINDOW):
        one = pltpu.make_async_copy(got_pack.at[k], pin.at[k], in_sem.at[k, 0])
        two = pltpu.make_async_copy(got_state.at[k], sin.at[k], in_sem.at[k, 1])
        one.start()
        two.start()
        loads.append((one, two))
    hidden_out[...] = hidden[...]
    chunk = 256
    slots = []
    for k in range(WINDOW):
        loads[k][0].wait()
        loads[k][1].wait()
        slot = jnp.max(pin[k, PACK_ROWS - 1 : PACK_ROWS, width : width + NSTATE].astype(F32)).astype(
            jnp.int32
        )
        slots.append(slot)

        @pl.when(slot >= 0)
        def _():
            def body(c, carry):
                rows = pl.ds(pl.multiple_of(c * chunk, chunk), chunk)
                sout[k, rows, :] = finish_rows(
                    sin[k, rows, :], pin[k, :, rows], pin[k, 0:8, width : width + NSTATE]
                )
                return carry

            lax.fori_loop(0, width // chunk, body, 0)
            kept_i[slot] = pin[k, 10:13, :width]
            kept_s[slot] = pin[k, 8:11, width:]
            pltpu.make_async_copy(sout.at[k], kept.at[slot], out_sem.at[k]).start()

    for k in range(WINDOW):

        @pl.when(slots[k] >= 0)
        def _():
            pltpu.make_async_copy(sout.at[k], kept.at[slots[k]], out_sem.at[k]).wait()


def local(
    peers,
    hidden_in,
    norm_gain,
    proj_gate,
    proj_inner,
    proj_ssm,
    proj_step,
    step_bias,
    decay_log,
    skip_gain,
    conv_inner,
    conv_inner_bias,
    conv_ssm,
    conv_ssm_bias,
    gate_gain,
    proj_out,
    states_in,
    edge_inner,
    edge_ssm,
    draft_lengths,
    accepted,
    destination,
):
    count, heads = states_in.shape[0], states_in.shape[1]
    rows, half = hidden_in.shape
    width = proj_gate.shape[1]
    model = proj_gate.shape[0]
    flat = states_in.reshape(count, width, NSTATE)
    pack_width = width + 2 * NSTATE
    smem = pl.BlockSpec(memory_space=pltpu.SMEM)
    vmem = pl.BlockSpec(memory_space=pltpu.VMEM)
    hbm = pl.BlockSpec(memory_space=pl.ANY)

    def line(value):
        return value.reshape(1, -1)

    got_state, got_pack, hidden_out = pl.pallas_call(
        functools.partial(layer_kernel, (peers, count, heads)),
        name="layer",
        out_shape=(
            jax.ShapeDtypeStruct((WINDOW, width, NSTATE), BF16),
            jax.ShapeDtypeStruct((WINDOW, PACK_ROWS, pack_width), BF16),
            jax.ShapeDtypeStruct((rows, half), BF16),
        ),
        in_specs=[smem] * 3 + [vmem] * 12 + [hbm] * 6,
        out_specs=(hbm, hbm, vmem),
        scratch_shapes=[
            pltpu.VMEM((model, width), BF16),
            pltpu.VMEM((model, width), BF16),
            pltpu.VMEM((model, NSTATE), BF16),
            pltpu.VMEM((model, heads), BF16),
            pltpu.VMEM((width, model), BF16),
            pltpu.VMEM((count, width, NSTATE), BF16),
            pltpu.VMEM((WINDOW, width, NSTATE), BF16),
            pltpu.VMEM((WINDOW, PACK_ROWS, pack_width), BF16),
            pltpu.VMEM((count, PACK_ROWS, pack_width), F32),
            pltpu.VMEM((2, rows, half), BF16),
            pltpu.VMEM((rows, model), BF16),
            pltpu.VMEM((count, 16, width), F32),
            pltpu.VMEM((count, 16, 2 * NSTATE), F32),
            pltpu.VMEM((rows, NSTATE), BF16),
            pltpu.VMEM((rows, NSTATE), BF16),
            pltpu.VMEM((rows, width), F32),
            pltpu.VMEM((rows, width), F32),
            pltpu.VMEM((8, heads), F32),
            pltpu.VMEM((8, width), F32),
            pltpu.VMEM((rows, width), F32),
            pltpu.VMEM((rows, NSTATE), F32),
            pltpu.VMEM((rows, NSTATE), F32),
            pltpu.VMEM((2, rows, half), F32),
            pltpu.VMEM((rows, half), F32),
            pltpu.SemaphoreType.DMA((8,)),
            pltpu.SemaphoreType.DMA((19,)),
            pltpu.SemaphoreType.DMA((19,)),
        ],
        compiler_params=pltpu.CompilerParams(
            collective_id=1, has_side_effects=True, vmem_limit_bytes=60 * 1024 * 1024
        ),
    )(
        draft_lengths,
        accepted,
        destination,
        hidden_in,
        line(norm_gain),
        line(step_bias),
        line(decay_log),
        line(skip_gain),
        conv_inner,
        line(conv_inner_bias),
        conv_ssm,
        line(conv_ssm_bias),
        line(gate_gain),
        edge_inner,
        edge_ssm,
        proj_gate,
        proj_inner,
        proj_ssm,
        proj_step,
        proj_out,
        flat,
    )
    kept, kept_i, kept_s, hidden = pl.pallas_call(
        functools.partial(place_kernel, (count, width)),
        name="place",
        out_shape=(
            jax.ShapeDtypeStruct(flat.shape, BF16),
            jax.ShapeDtypeStruct(edge_inner.shape, BF16),
            jax.ShapeDtypeStruct(edge_ssm.shape, BF16),
            jax.ShapeDtypeStruct(hidden_in.shape, BF16),
        ),
        in_specs=[hbm, hbm, vmem],
        out_specs=(hbm, vmem, vmem, vmem),
        scratch_shapes=[
            pltpu.VMEM((WINDOW, width, NSTATE), BF16),
            pltpu.VMEM((WINDOW, PACK_ROWS, pack_width), BF16),
            pltpu.VMEM((WINDOW, width, NSTATE), BF16),
            pltpu.VMEM((8, 128), F32),
            pltpu.VMEM((8, 128), F32),
            pltpu.SemaphoreType.DMA((WINDOW, 2)),
            pltpu.SemaphoreType.DMA((WINDOW,)),
        ],
    )(got_state, got_pack, hidden_out)
    return (hidden, kept.reshape(states_in.shape), kept_i, kept_s)


def solution(mesh):
    in_specs = (
        P("req", "head"),
        P(),
        P(None, "head"),
        P(None, "head"),
        P(None, "head"),
        P(None, "head"),
        P("head"),
        P("head"),
        P("head"),
        P(None, "head"),
        P("head"),
        P(),
        P(),
        P("head"),
        P("head", None),
        P("req", "head", None, None),
        P("req", None, "head"),
        P("req", None, None),
        P("req"),
        P("req"),
        P("req"),
    )
    out_specs = (
        P("req", "head"),
        P("req", "head", None, None),
        P("req", None, "head"),
        P("req", None, None),
    )
    return jax.shard_map(
        functools.partial(local, mesh.shape["req"]),
        mesh=mesh,
        in_specs=in_specs,
        out_specs=out_specs,
        check_vma=False,
    )
```

```python
import functools

import jax
import jax.numpy as jnp
from jax import lax
from jax.experimental import pallas as pl
from jax.experimental.pallas import tpu as pltpu
from jax.sharding import PartitionSpec as P

HEAD_DIM = 64
NSTATE = 128
KCONV = 4
DRAFT = 8
WINDOW = 8
DINNER = 3072
EPS = 1e-05
MESH = pl.DeviceIdType.MESH
F32 = jnp.float32
BF16 = jnp.bfloat16
PACK_ROWS = 16


def silu(value):
    return value * jax.nn.sigmoid(value)


def finish_state(state, factors, store):
    width = factors.shape[1] - NSTATE
    row = lax.broadcasted_iota(jnp.int32, (PACK_ROWS, NSTATE), 0)
    decay = jnp.where((row == 8) | (row == 9), 1.0, 0.0).astype(BF16)
    right = jnp.concatenate([factors[:, width:], decay], axis=1)
    chunk = 512
    for c in range(0, width, chunk):
        both = lax.dot_general(
            factors[:, c : c + chunk], right, (((0,), (0,)), ((), ())), preferred_element_type=F32
        )
        store(c, chunk, (state(c, chunk).astype(F32) * both[:, NSTATE:] + both[:, :NSTATE]).astype(BF16))


RAW = (7, 6, 5)
KEPT = (3, 4, 2, 1)
PIECES = {0: ((0, 1536),), 1: ((0, 768), (768, 768)), 2: ((0, 320), (320, 320), (640, 896))}
OFFSETS = (1, 2, 3, 4, 5, 6, 7, 8, -1, -2, -3, -13, -14, -15, 17, 18, 19, 20, -12)
ROW_LEN, COL_LEN = 4, 8


class Wires:
    def __init__(self, peers, me, head, send_sem, recv_sem):
        self.peers, self.me, self.head = peers, me, head
        self.send_sem, self.recv_sem = send_sem, recv_sem
        self.x = lax.rem(me, ROW_LEN)
        self.y = lax.rem(lax.div(me, ROW_LEN), COL_LEN)
        self.sent = []

    def at(self, offset):
        return {"req": lax.rem(self.me + offset + self.peers, self.peers), "head": self.head}

    def copy(self, src, dst, i, device, out=None):
        return pltpu.make_async_remote_copy(
            src_ref=src,
            dst_ref=dst,
            send_sem=self.send_sem.at[i if out is None else out],
            recv_sem=self.recv_sem.at[i],
            device_id=device,
            device_id_type=MESH,
        )

    def go(self, cond, src, dst, i, device, out=None):
        copy = self.copy(src, dst, i, device, out)
        if cond is True:
            copy.start()
        else:
            pl.when(cond)(copy.start)
        self.sent.append((cond, copy))

    def steps_of(self, k, column):
        cases = sorted({(x + k) // ROW_LEN for x in range(ROW_LEN)})
        steps = lax.div(column + k, ROW_LEN)
        return [(True if len(cases) == 1 else steps == d, d) for d in cases]

    def source_column(self, k):
        return lax.rem(self.x + 2 * ROW_LEN - k, ROW_LEN)

    def up(self, turn):
        if turn > 0:
            return jnp.where(self.y >= 3, -3 * ROW_LEN, (COL_LEN - 3) * ROW_LEN)
        return jnp.where(self.y < COL_LEN - 3, 3 * ROW_LEN, -(COL_LEN - 3) * ROW_LEN)

    def start_relayed(self, k, src, relay):
        if k == ROW_LEN:
            return
        for cond, d in self.steps_of(k, self.x):
            if d == 2:
                rows = pl.ds(*PIECES[d][2])
                self.go(cond, src.at[rows], relay.at[rows], 40 + k, self.at(self.up(1) + k - d * ROW_LEN))
            if d > 0:
                rows = pl.ds(*PIECES[d][1])
                self.go(cond, src.at[rows], relay.at[rows], 24 + k, self.at(k - d * ROW_LEN), 88 + 8 * d + k)

    def start_direct(self, k, src, dst):
        if k == ROW_LEN:
            self.go(True, src, dst, 8 + k, self.at(k))
            return
        for cond, d in self.steps_of(k, self.x):
            rows = pl.ds(*PIECES[d][0])
            self.go(cond, src.at[rows], dst.at[rows], 8 + k, self.at(k), 112 + 8 * d + k)

    def pass_on(self, k, relay, dst):
        for cond, d in self.steps_of(k, self.source_column(k)):
            if d == 0:
                continue
            rows = pl.ds(*PIECES[d][1])

            def wait():
                self.copy(relay.at[rows], relay.at[rows], 24 + k, self.at(1)).wait_recv()

            if cond is True:
                wait()
            else:
                pl.when(cond)(wait)
            self.go(cond, relay.at[rows], dst.at[rows], 16 + k, self.at(d * ROW_LEN), 56 + 8 * d + k)

    def pass_round(self, k, relay, dst):
        for cond, d in self.steps_of(k, self.source_column(k)):
            if d != 2:
                continue
            rows = pl.ds(*PIECES[d][2])

            def wait():
                self.copy(relay.at[rows], relay.at[rows], 40 + k, self.at(1)).wait_recv()

            if cond is True:
                wait()
            else:
                pl.when(cond)(wait)
            self.go(cond, relay.at[rows], dst.at[rows], 32 + k, self.at(self.up(-1) + 2 * ROW_LEN), 80 + k)

    def arrive(self, k, dst):
        if k == ROW_LEN:
            self.copy(dst, dst, 8 + k, self.at(1)).wait_recv()
            return
        for cond, d in self.steps_of(k, self.source_column(k)):

            def wait():
                for i, piece in enumerate(PIECES[d]):
                    rows = pl.ds(*piece)
                    self.copy(dst.at[rows], dst.at[rows], 8 + 8 * i + k if i < 2 else 32 + k, self.at(1)).wait_recv()

            if cond is True:
                wait()
            else:
                pl.when(cond)(wait)

    def drain(self):
        for cond, copy in self.sent:
            if cond is True:
                copy.wait_send()
            else:
                pl.when(cond)(copy.wait_send)


def layer_kernel(
    sizes,
    lengths,
    accepted,
    destination,
    hid,
    norm_gain,
    step_bias,
    decay_log,
    skip_gain,
    conv_i,
    bias_i,
    conv_s,
    bias_s,
    gate_gain,
    edge_i,
    edge_s,
    wg_hbm,
    wi_hbm,
    ws_hbm,
    wt_hbm,
    wo_hbm,
    st_hbm,
    got_state,
    got_edge,
    hidden_out,
    wg,
    wi,
    ws,
    wt,
    wo,
    st,
    send,
    raw,
    done,
    relay,
    packs,
    got_pack,
    edges,
    pack_f,
    pack_b,
    edge_f,
    lines,
    whole,
    nrm,
    seq_i,
    seq_s,
    ssm_own,
    ssm_got,
    gate,
    steps,
    vec,
    vec_x,
    gated,
    sq_own,
    sq_got,
    part,
    part_got,
    local_sem,
    send_sem,
    recv_sem,
):
    peers, count, heads = sizes
    rows = count * DRAFT
    half = hid.shape[1]
    width = wg.shape[1]
    me = lax.axis_index("req")
    head = lax.axis_index("head")
    other = 1 - head

    local = []
    for i, (src, dst) in enumerate(
        (
            (st_hbm, st),
            (ws_hbm, ws),
            (wt_hbm, wt),
            (wi_hbm, wi),
            (wg_hbm, wg),
            (wo_hbm, wo),
        )
    ):
        copy = pltpu.make_async_copy(src, dst, local_sem.at[i])
        copy.start()
        local.append(copy)

    wires = Wires(peers, me, head, send_sem, recv_sem)
    partner = {"req": me, "head": other}
    barrier = pltpu.get_barrier_semaphore()
    for offset in OFFSETS:
        pl.semaphore_signal(barrier, inc=1, device_id=wires.at(-offset), device_id_type=MESH)
    pl.semaphore_signal(barrier, inc=1, device_id=partner, device_id_type=MESH)
    pl.semaphore_wait(barrier, len(OFFSETS) + 1)

    to_partner = wires.copy(hid, whole.at[head], 0, partner)
    to_partner.start()

    reach, slots = [], []
    for r in range(count):
        target = destination[r]
        owner = lax.div(target, count)
        reach.append(lax.rem(owner - me + peers, peers))
        slots.append(target - owner * count)
    picks, valid = [], []
    for k in range(WINDOW):
        pick = jnp.int32(0)
        found = jnp.int32(0)
        for r in range(count):
            hit = reach[r] == k
            pick = jnp.where(hit, jnp.int32(r), pick)
            found = jnp.where(hit, jnp.int32(1), found)
        picks.append(pick)
        valid.append(found)

    local[0].wait()
    for k in RAW:
        send[k] = st[picks[k]]
    for k in RAW:
        wires.start_relayed(k, send.at[k], relay.at[k])
    for k in RAW:
        wires.start_direct(k, send.at[k], raw.at[k - RAW[-1]])

    for i in range(width // 128):
        cols = slice(i * 128, (i + 1) * 128)
        lines[0:1, cols] = norm_gain[i : i + 1, :]
        lines[1:2, cols] = bias_i[i : i + 1, :]
        lines[2:3, cols] = gate_gain[i : i + 1, :]
    whole[pl.ds(head, 1)] = hid[...][None]
    to_partner.wait()
    left = whole[0].astype(F32)
    right = whole[1].astype(F32)
    mean = (
        jnp.sum(left * left, axis=-1, keepdims=True) + jnp.sum(right * right, axis=-1, keepdims=True)
    ) / (2 * half)
    scale = lax.rsqrt(mean + EPS)
    nrm[:, :half] = (left * scale * lines[0:1, :half]).astype(BF16)
    nrm[:, half:] = (right * scale * lines[0:1, half:]).astype(BF16)

    local[1].wait()
    ssm_own[...] = jnp.dot(nrm[...], ws[...], preferred_element_type=F32).astype(BF16)
    ssm_move = wires.copy(ssm_own, ssm_got, 1, partner)
    ssm_move.start()

    spread = (
        lax.shift_right_logical(lax.broadcasted_iota(jnp.int32, (heads, width), 1), 6)
        == lax.broadcasted_iota(jnp.int32, (heads, width), 0)
    ).astype(F32)
    vec[...] = jnp.zeros_like(vec)
    vec[0:1, :] = step_bias[...]
    vec[1:2, :] = decay_log[...]
    vec[2:3, :] = skip_gain[...]
    vec_x[...] = jnp.dot(
        vec[...], spread, precision=lax.Precision.HIGHEST, preferred_element_type=F32
    )
    local[2].wait()
    step_raw = lax.dot_general(
        nrm[...], wt[...], (((1,), (1,)), ((), ())), preferred_element_type=F32
    ).astype(BF16)
    step_x = jnp.dot(step_raw, spread.astype(BF16), preferred_element_type=F32) + vec_x[0:1, :]
    steps[...] = jnp.maximum(step_x, 0.0) + jnp.log1p(jnp.exp(-jnp.abs(step_x)))

    tile = 256
    local[3].wait()

    def project_inner(j, carry):
        cols = pl.ds(pl.multiple_of(j * tile, tile), tile)
        value = jnp.dot(nrm[...], wi[:, cols], preferred_element_type=F32)
        value = value.astype(BF16).astype(F32)
        for r in range(count):
            seq_i[r, 8:16, cols] = value[r * DRAFT : (r + 1) * DRAFT]
        return carry

    lax.fori_loop(0, width // tile, project_inner, 0)
    local[4].wait()

    def project_gate(j, carry):
        cols = pl.ds(pl.multiple_of(j * tile, tile), tile)
        value = jnp.dot(nrm[...], wg[:, cols], preferred_element_type=F32)
        value = value.astype(BF16).astype(F32)
        gate[:, cols] = silu(value)
        return carry

    lax.fori_loop(0, width // tile, project_gate, 0)

    for k in RAW:
        wires.pass_on(k, relay.at[k], raw.at[k - RAW[-1]])

    ssm_move.wait()
    own_cols = ssm_own[...].astype(F32)
    got_cols = ssm_got[...].astype(F32)
    first = head == 0
    bcols = jnp.where(first, own_cols, got_cols)
    ccols = jnp.where(first, got_cols, own_cols)
    for r in range(count):
        seq_i[r, 5:8, :] = edge_i[r].astype(F32)
        seq_s[r, 5:8, :] = edge_s[r].astype(F32)
        seq_s[r, 8:16, :NSTATE] = bcols[r * DRAFT : (r + 1) * DRAFT]
        seq_s[r, 8:16, NSTATE:] = ccols[r * DRAFT : (r + 1) * DRAFT]

    slot_of = slots

    def one_request(r, carry):
        block = pl.ds(pl.multiple_of(r * DRAFT, DRAFT), DRAFT)
        total = jnp.zeros((DRAFT, width), F32) + lines[1:2, :]
        narrow = jnp.zeros((DRAFT, 2 * NSTATE), F32) + bias_s[...]
        for k in range(KCONV):
            total = total + seq_i[r, 5 + k : 13 + k, :] * conv_i[k : k + 1, :].astype(F32)
            narrow = narrow + seq_s[r, 5 + k : 13 + k, :] * conv_s[k : k + 1, :].astype(F32)
        x = silu(total).astype(BF16).astype(F32)
        bc = silu(narrow).astype(BF16)
        bmat, cmat = bc[:, :NSTATE], bc[:, NSTATE:]
        when = lax.broadcasted_iota(jnp.int32, (DRAFT, width), 0)
        step = jnp.where(when < lengths[r], steps[block, :], 0.0)
        change = step * -jnp.exp(vec_x[1:2, :])
        decay = change
        for shift in (1, 2, 4):
            decay = decay + jnp.where(when >= shift, pltpu.roll(decay, shift, 0), 0.0)
        weighted = step * x
        pair = lax.dot_general(cmat, bmat, (((1,), (1,)), ((), ())), preferred_element_type=F32)
        seen = lax.dot_general(cmat, st[r], (((1,), (1,)), ((), ())), preferred_element_type=F32)
        out = jnp.exp(decay) * seen + vec_x[2:3, :] * x
        for u in range(DRAFT):
            lag = jnp.where(when >= u, decay - decay[u : u + 1, :], -1e30)
            out = out + jnp.exp(lag) * pair[:, u : u + 1] * weighted[u : u + 1, :]
        ssm_out = out.astype(BF16).astype(F32)
        value = ssm_out * gate[block, :]
        gated[block, :] = value
        sq_own[block, :] = jnp.broadcast_to(
            jnp.sum(value * value, axis=-1, keepdims=True), (DRAFT, NSTATE)
        )
        taken = accepted[r]
        end = jnp.sum(jnp.where(when < taken, change, 0.0), axis=0, keepdims=True)
        lag = jnp.where(when < taken, end - decay, -1e30)
        pack_f[r, 0:8, :width] = jnp.exp(lag) * weighted
        whole_decay = jnp.exp(end)
        high = whole_decay.astype(BF16).astype(F32)
        pack_f[r, 8:9, :width] = high
        pack_f[r, 9:10, :width] = whole_decay - high
        pack_f[r, 10:16, :width] = jnp.zeros((6, width), F32)
        pack_f[r, 0:8, width:] = bmat.astype(F32)
        pack_f[r, 8:16, width:] = jnp.zeros((8, NSTATE), F32)
        pack_b[r] = pack_f[r].astype(BF16)
        for i in range(KCONV - 1):
            edge_f[r, i : i + 1, :width] = seq_i[r, pl.ds(5 + taken + i, 1), :]
            edge_f[r, i : i + 1, width:] = seq_s[r, pl.ds(5 + taken + i, 1), :]
        slot = slot_of[0]
        for q in range(1, count):
            slot = jnp.where(r == q, slot_of[q], slot)
        edge_f[r, 3:4, :] = jnp.zeros((1, width + 2 * NSTATE), F32) + slot.astype(F32)
        return carry

    lax.fori_loop(0, count, one_request, 0)

    sq_move = wires.copy(sq_own, sq_got, 2, partner)
    sq_move.start()
    for k in RAW:
        packs[k - RAW[-1]] = pack_b[picks[k]]
    for k in RAW:
        wires.go(True, packs.at[k - RAW[-1]], got_pack.at[k - RAW[-1]], 48 + k, wires.at(k))

    def keep(k):
        def state(c, n):
            return st[picks[k], pl.ds(c, n), :]

        def store(c, n, value):
            send[k, pl.ds(c, n), :] = value

        finish_state(state, pack_b[picks[k]], store)

    for k in KEPT:
        keep(k)
        wires.start_relayed(k, send.at[k], relay.at[k])
        wires.start_direct(k, send.at[k], got_state.at[k])
    for k in range(WINDOW):
        edges[k] = jnp.where(valid[k] > 0, edge_f[picks[k]], -1.0).astype(BF16)
    for k in range(1, WINDOW):
        wires.go(True, edges.at[k], got_edge.at[k], 56 + k, wires.at(k))
    for k in RAW:
        wires.pass_round(k, relay.at[k], raw.at[k - RAW[-1]])
    keep(0)
    own_state = pltpu.make_async_copy(send.at[0], got_state.at[0], local_sem.at[6])
    own_state.start()
    own_edge = pltpu.make_async_copy(edges.at[0], got_edge.at[0], local_sem.at[7])
    own_edge.start()

    sq_move.wait()
    square = (sq_own[:, 0:1] + sq_got[:, 0:1]) / DINNER
    nrm[...] = (gated[...] * lax.rsqrt(square + EPS) * lines[2:3, :]).astype(BF16)

    local[5].wait()
    per = half // tile

    def project_out(j, carry):
        which = jnp.where(j < per, other, head)
        i = jnp.where(j < per, j, j - per)
        cols = pl.ds(pl.multiple_of(which * half + i * tile, tile), tile)
        value = jnp.dot(nrm[...], wo[:, cols], preferred_element_type=F32)
        part[pl.ds(jnp.where(j < per, 0, 1), 1), :, pl.ds(pl.multiple_of(i * tile, tile), tile)] = value[None]
        return carry

    lax.fori_loop(0, per, project_out, 0)
    part_move = wires.copy(part.at[0], part_got, 3, partner)
    part_move.start()
    lax.fori_loop(per, 2 * per, project_out, 0)
    for k in KEPT:
        if k != ROW_LEN:
            wires.pass_on(k, relay.at[k], got_state.at[k])
    part_move.wait()
    hidden_out[...] = (hid[...].astype(F32) + part[1] + part_got[...]).astype(BF16)

    finals = [own_state, own_edge]
    for k in RAW:
        i = k - RAW[-1]
        wires.copy(packs.at[i], got_pack.at[i], 48 + k, wires.at(1)).wait_recv()
        wires.arrive(k, raw.at[i])

        def state(c, n):
            return raw[i, pl.ds(c, n), :]

        def store(c, n, value):
            done[i, pl.ds(c, n), :] = value

        finish_state(state, got_pack[i], store)
        copy = pltpu.make_async_copy(done.at[i], got_state.at[k], local_sem.at[8 + i])
        copy.start()
        finals.append(copy)
    for k in KEPT:
        wires.arrive(k, got_state.at[k])
    for k in range(1, WINDOW):
        wires.copy(edges.at[k], got_edge.at[k], 56 + k, wires.at(1)).wait_recv()
    wires.drain()
    for copy in finals:
        copy.wait()


def place_kernel(sizes, got_state, got_edge, hidden, kept, kept_i, kept_s, hidden_out, buf, in_sem, out_sem):
    count, width = sizes
    loads = []
    for k in range(WINDOW):
        copy = pltpu.make_async_copy(got_state.at[k], buf.at[k], in_sem.at[k])
        copy.start()
        loads.append(copy)
    hidden_out[...] = hidden[...]
    slots = []
    for k in range(WINDOW):
        slots.append(jnp.max(got_edge[k, 3:4, :128].astype(F32)).astype(jnp.int32))
    for k in range(WINDOW):
        loads[k].wait()

        @pl.when(slots[k] >= 0)
        def _():
            pltpu.make_async_copy(buf.at[k], kept.at[slots[k]], out_sem.at[k]).start()
            kept_i[slots[k]] = got_edge[k, 0:3, :width]
            kept_s[slots[k]] = got_edge[k, 0:3, width:]

    for k in range(WINDOW):

        @pl.when(slots[k] >= 0)
        def _():
            pltpu.make_async_copy(buf.at[k], kept.at[slots[k]], out_sem.at[k]).wait()


def local(
    peers,
    hidden_in,
    norm_gain,
    proj_gate,
    proj_inner,
    proj_ssm,
    proj_step,
    step_bias,
    decay_log,
    skip_gain,
    conv_inner,
    conv_inner_bias,
    conv_ssm,
    conv_ssm_bias,
    gate_gain,
    proj_out,
    states_in,
    edge_inner,
    edge_ssm,
    draft_lengths,
    accepted,
    destination,
):
    count, heads = states_in.shape[0], states_in.shape[1]
    rows, half = hidden_in.shape
    width = proj_gate.shape[1]
    model = proj_gate.shape[0]
    flat = states_in.reshape(count, width, NSTATE)
    pack_width = width + NSTATE
    edge_width = width + 2 * NSTATE
    raws = len(RAW)
    smem = pl.BlockSpec(memory_space=pltpu.SMEM)
    vmem = pl.BlockSpec(memory_space=pltpu.VMEM)
    hbm = pl.BlockSpec(memory_space=pl.ANY)

    def line(value):
        return value.reshape(1, -1)

    def tiled(value):
        return value.reshape(-1, 128)

    got_state, got_edge, hidden_out = pl.pallas_call(
        functools.partial(layer_kernel, (peers, count, heads)),
        name="layer",
        out_shape=(
            jax.ShapeDtypeStruct((WINDOW, width, NSTATE), BF16),
            jax.ShapeDtypeStruct((WINDOW, 4, edge_width), BF16),
            jax.ShapeDtypeStruct((rows, half), BF16),
        ),
        in_specs=[smem] * 3 + [vmem] * 12 + [hbm] * 6,
        out_specs=(hbm, hbm, vmem),
        scratch_shapes=[
            pltpu.VMEM((model, width), BF16),
            pltpu.VMEM((model, width), BF16),
            pltpu.VMEM((model, NSTATE), BF16),
            pltpu.VMEM((heads, model), BF16),
            pltpu.VMEM((width, model), BF16),
            pltpu.VMEM((count, width, NSTATE), BF16),
            pltpu.VMEM((WINDOW, width, NSTATE), BF16),
            pltpu.VMEM((raws, width, NSTATE), BF16),
            pltpu.VMEM((raws, width, NSTATE), BF16),
            pltpu.VMEM((WINDOW, width, NSTATE), BF16),
            pltpu.VMEM((raws, PACK_ROWS, pack_width), BF16),
            pltpu.VMEM((raws, PACK_ROWS, pack_width), BF16),
            pltpu.VMEM((WINDOW, 4, edge_width), BF16),
            pltpu.VMEM((count, PACK_ROWS, pack_width), F32),
            pltpu.VMEM((count, PACK_ROWS, pack_width), BF16),
            pltpu.VMEM((count, 4, edge_width), F32),
            pltpu.VMEM((8, width), F32),
            pltpu.VMEM((2, rows, half), BF16),
            pltpu.VMEM((rows, model), BF16),
            pltpu.VMEM((count, 16, width), F32),
            pltpu.VMEM((count, 16, 2 * NSTATE), F32),
            pltpu.VMEM((rows, NSTATE), BF16),
            pltpu.VMEM((rows, NSTATE), BF16),
            pltpu.VMEM((rows, width), F32),
            pltpu.VMEM((rows, width), F32),
            pltpu.VMEM((8, heads), F32),
            pltpu.VMEM((8, width), F32),
            pltpu.VMEM((rows, width), F32),
            pltpu.VMEM((rows, NSTATE), F32),
            pltpu.VMEM((rows, NSTATE), F32),
            pltpu.VMEM((2, rows, half), F32),
            pltpu.VMEM((rows, half), F32),
            pltpu.SemaphoreType.DMA((12,)),
            pltpu.SemaphoreType.DMA((144,)),
            pltpu.SemaphoreType.DMA((64,)),
        ],
        compiler_params=pltpu.CompilerParams(
            collective_id=1, has_side_effects=True, vmem_limit_bytes=60 * 1024 * 1024
        ),
    )(
        draft_lengths,
        accepted,
        destination,
        hidden_in,
        tiled(norm_gain),
        line(step_bias),
        line(decay_log),
        line(skip_gain),
        conv_inner,
        tiled(conv_inner_bias),
        conv_ssm,
        line(conv_ssm_bias),
        tiled(gate_gain),
        edge_inner,
        edge_ssm,
        proj_gate,
        proj_inner,
        proj_ssm,
        proj_step.T,
        proj_out,
        flat,
    )
    kept, kept_i, kept_s, hidden = pl.pallas_call(
        functools.partial(place_kernel, (count, width)),
        name="place",
        out_shape=(
            jax.ShapeDtypeStruct(flat.shape, BF16),
            jax.ShapeDtypeStruct(edge_inner.shape, BF16),
            jax.ShapeDtypeStruct(edge_ssm.shape, BF16),
            jax.ShapeDtypeStruct(hidden_in.shape, BF16),
        ),
        in_specs=[hbm, vmem, vmem],
        out_specs=(hbm, vmem, vmem, vmem),
        scratch_shapes=[
            pltpu.VMEM((WINDOW, width, NSTATE), BF16),
            pltpu.SemaphoreType.DMA((WINDOW,)),
            pltpu.SemaphoreType.DMA((WINDOW,)),
        ],
    )(got_state, got_edge, hidden_out)
    return (hidden, kept.reshape(states_in.shape), kept_i, kept_s)


def solution(mesh):
    in_specs = (
        P("req", "head"),
        P(),
        P(None, "head"),
        P(None, "head"),
        P(None, "head"),
        P(None, "head"),
        P("head"),
        P("head"),
        P("head"),
        P(None, "head"),
        P("head"),
        P(),
        P(),
        P("head"),
        P("head", None),
        P("req", "head", None, None),
        P("req", None, "head"),
        P("req", None, None),
        P("req"),
        P("req"),
        P("req"),
    )
    out_specs = (
        P("req", "head"),
        P("req", "head", None, None),
        P("req", None, "head"),
        P("req", None, None),
    )
    return jax.shard_map(
        functools.partial(local, mesh.shape["req"]),
        mesh=mesh,
        in_specs=in_specs,
        out_specs=out_specs,
        check_vma=False,
    )
```

```python
import functools

import jax
import jax.numpy as jnp
from jax import lax
from jax.experimental import pallas as pl
from jax.experimental.pallas import tpu as pltpu
from jax.sharding import PartitionSpec as P

HEAD_DIM = 64
NSTATE = 128
KCONV = 4
DRAFT = 8
WINDOW = 8
DINNER = 3072
EPS = 1e-05
MESH = pl.DeviceIdType.MESH
F32 = jnp.float32
BF16 = jnp.bfloat16
PACK_ROWS = 16


def silu(value):
    return value * jax.nn.sigmoid(value)


def finish_state(state, factors, store):
    width = factors.shape[1] - NSTATE
    row = lax.broadcasted_iota(jnp.int32, (PACK_ROWS, NSTATE), 0)
    decay = jnp.where((row == 8) | (row == 9), 1.0, 0.0).astype(BF16)
    right = jnp.concatenate([factors[:, pl.ds(width, NSTATE)], decay], axis=1)
    chunk = 512

    def part(i, carry):
        rows = pl.ds(pl.multiple_of(i * chunk, chunk), chunk)
        both = lax.dot_general(
            factors[:, rows], right, (((0,), (0,)), ((), ())), preferred_element_type=F32
        )
        store(rows, (state(rows).astype(F32) * both[:, NSTATE:] + both[:, :NSTATE]).astype(BF16))
        return carry

    lax.fori_loop(0, width // chunk, part, 0)


ORDER = (7, 6, 5, 3, 4, 2, 1)
EARLY = 2
PIECES = {0: ((0, 1536),), 1: ((0, 768), (768, 768)), 2: ((0, 512), (512, 512), (1024, 512))}
OFFSETS = (1, 2, 3, 4, 5, 6, 7, 8, -1, -2, -3, -13, -14, -15, 17, 18, 19, 20, -12)
ROW_LEN, COL_LEN = 4, 8


class Wires:
    def __init__(self, peers, me, head, send_sem, recv_sem):
        self.peers, self.me, self.head = peers, me, head
        self.send_sem, self.recv_sem = send_sem, recv_sem
        self.x = lax.rem(me, ROW_LEN)
        self.y = lax.rem(lax.div(me, ROW_LEN), COL_LEN)
        self.sent = []

    def at(self, offset):
        return {"req": lax.rem(self.me + offset + self.peers, self.peers), "head": self.head}

    def copy(self, src, dst, i, device, out=None):
        return pltpu.make_async_remote_copy(
            src_ref=src,
            dst_ref=dst,
            send_sem=self.send_sem.at[i if out is None else out],
            recv_sem=self.recv_sem.at[i],
            device_id=device,
            device_id_type=MESH,
        )

    def go(self, cond, src, dst, i, device, out=None):
        copy = self.copy(src, dst, i, device, out)
        if cond is True:
            copy.start()
        else:
            pl.when(cond)(copy.start)
        self.sent.append((cond, copy))

    def steps_of(self, k, column):
        cases = sorted({(x + k) // ROW_LEN for x in range(ROW_LEN)})
        steps = lax.div(column + k, ROW_LEN)
        return [(True if len(cases) == 1 else steps == d, d) for d in cases]

    def source_column(self, k):
        return lax.rem(self.x + 2 * ROW_LEN - k, ROW_LEN)

    def up(self, turn):
        if turn > 0:
            return jnp.where(self.y >= 3, -3 * ROW_LEN, (COL_LEN - 3) * ROW_LEN)
        return jnp.where(self.y < COL_LEN - 3, 3 * ROW_LEN, -(COL_LEN - 3) * ROW_LEN)

    def start_relayed(self, k, src, relay):
        if k == ROW_LEN:
            return
        for cond, d in self.steps_of(k, self.x):
            if d == 2:
                rows = pl.ds(*PIECES[d][2])
                self.go(cond, src.at[rows], relay.at[rows], 40 + k, self.at(self.up(1) + k - d * ROW_LEN))
            if d > 0:
                rows = pl.ds(*PIECES[d][1])
                self.go(cond, src.at[rows], relay.at[rows], 24 + k, self.at(k - d * ROW_LEN), 88 + 8 * d + k)

    def start_direct(self, k, src, dst):
        if k == ROW_LEN:
            self.go(True, src, dst, 8 + k, self.at(k))
            return
        for cond, d in self.steps_of(k, self.x):
            rows = pl.ds(*PIECES[d][0])
            self.go(cond, src.at[rows], dst.at[rows], 8 + k, self.at(k), 112 + 8 * d + k)

    def pass_on(self, k, relay, dst):
        for cond, d in self.steps_of(k, self.source_column(k)):
            if d == 0:
                continue
            rows = pl.ds(*PIECES[d][1])

            def wait():
                self.copy(relay.at[rows], relay.at[rows], 24 + k, self.at(1)).wait_recv()

            if cond is True:
                wait()
            else:
                pl.when(cond)(wait)
            self.go(cond, relay.at[rows], dst.at[rows], 16 + k, self.at(d * ROW_LEN), 56 + 8 * d + k)

    def pass_round(self, k, relay, dst):
        for cond, d in self.steps_of(k, self.source_column(k)):
            if d != 2:
                continue
            rows = pl.ds(*PIECES[d][2])

            def wait():
                self.copy(relay.at[rows], relay.at[rows], 40 + k, self.at(1)).wait_recv()

            if cond is True:
                wait()
            else:
                pl.when(cond)(wait)
            self.go(cond, relay.at[rows], dst.at[rows], 32 + k, self.at(self.up(-1) + 2 * ROW_LEN), 80 + k)

    def arrive(self, k, dst):
        if k == ROW_LEN:
            self.copy(dst, dst, 8 + k, self.at(1)).wait_recv()
            return
        for cond, d in self.steps_of(k, self.source_column(k)):

            def wait():
                for i, piece in enumerate(PIECES[d]):
                    rows = pl.ds(*piece)
                    self.copy(dst.at[rows], dst.at[rows], 8 + 8 * i + k if i < 2 else 32 + k, self.at(1)).wait_recv()

            if cond is True:
                wait()
            else:
                pl.when(cond)(wait)

    def drain(self):
        for cond, copy in self.sent:
            if cond is True:
                copy.wait_send()
            else:
                pl.when(cond)(copy.wait_send)


def layer_kernel(
    sizes,
    lengths,
    accepted,
    destination,
    hid,
    norm_gain,
    step_bias,
    decay_log,
    skip_gain,
    conv_i,
    bias_i,
    conv_s,
    bias_s,
    gate_gain,
    edge_i,
    edge_s,
    wg_hbm,
    wi_hbm,
    ws_hbm,
    wt_hbm,
    wo_hbm,
    st_hbm,
    got_state,
    got_edge,
    hidden_out,
    wg,
    wi,
    ws,
    wt,
    wo,
    st,
    send,
    raw,
    done,
    relay,
    packs,
    got_pack,
    edges,
    pack_f,
    pack_b,
    spare,
    edge_f,
    lines,
    whole,
    nrm,
    seq_i,
    seq_s,
    ssm_own,
    ssm_got,
    gate,
    steps,
    vec,
    vec_x,
    gated,
    sq_own,
    sq_got,
    part,
    part_got,
    local_sem,
    send_sem,
    recv_sem,
):
    peers, count, heads, active = sizes
    early, late = active[:EARLY], active[EARLY:]
    rows = count * DRAFT
    half = hid.shape[1]
    width = wg.shape[1]
    me = lax.axis_index("req")
    head = lax.axis_index("head")
    other = 1 - head

    local = []
    for i, (src, dst) in enumerate(
        (
            (st_hbm, st),
            (ws_hbm, ws),
            (wt_hbm, wt),
            (wi_hbm, wi),
            (wg_hbm, wg),
            (wo_hbm, wo),
        )
    ):
        copy = pltpu.make_async_copy(src, dst, local_sem.at[i])
        copy.start()
        local.append(copy)

    wires = Wires(peers, me, head, send_sem, recv_sem)
    partner = {"req": me, "head": other}
    barrier = pltpu.get_barrier_semaphore()
    for offset in OFFSETS:
        pl.semaphore_signal(barrier, inc=1, device_id=wires.at(-offset), device_id_type=MESH)
    pl.semaphore_signal(barrier, inc=1, device_id=partner, device_id_type=MESH)
    pl.semaphore_wait(barrier, len(OFFSETS) + 1)

    to_partner = wires.copy(hid, whole.at[head], 0, partner)
    to_partner.start()

    reach, slots = [], []
    for r in range(count):
        target = destination[r]
        owner = lax.div(target, count)
        reach.append(lax.rem(owner - me + peers, peers))
        slots.append(target - owner * count)
    picks, valid = [], []
    for k in range(WINDOW):
        pick = jnp.int32(0)
        found = jnp.int32(0)
        for r in range(count):
            hit = reach[r] == k
            pick = jnp.where(hit, jnp.int32(r), pick)
            found = jnp.where(hit, jnp.int32(1), found)
        picks.append(pick)
        valid.append(found)

    local[0].wait()
    for k in early:
        send[k] = st[picks[k]]
    for k in early:
        wires.start_relayed(k, send.at[k], relay.at[k])
    for k in early:
        wires.start_direct(k, send.at[k], raw.at[early.index(k)])

    for i in range(width // 128):
        cols = slice(i * 128, (i + 1) * 128)
        lines[0:1, cols] = norm_gain[i : i + 1, :]
        lines[1:2, cols] = bias_i[i : i + 1, :]
        lines[2:3, cols] = gate_gain[i : i + 1, :]
    whole[pl.ds(head, 1)] = hid[...][None]
    to_partner.wait()
    left = whole[0].astype(F32)
    right = whole[1].astype(F32)
    mean = (
        jnp.sum(left * left, axis=-1, keepdims=True) + jnp.sum(right * right, axis=-1, keepdims=True)
    ) / (2 * half)
    scale = lax.rsqrt(mean + EPS)
    nrm[:, :half] = (left * scale * lines[0:1, :half]).astype(BF16)
    nrm[:, half:] = (right * scale * lines[0:1, half:]).astype(BF16)

    local[1].wait()
    ssm_own[...] = jnp.dot(nrm[...], ws[...], preferred_element_type=F32).astype(BF16)
    ssm_move = wires.copy(ssm_own, ssm_got, 1, partner)
    ssm_move.start()

    spread = (
        lax.shift_right_logical(lax.broadcasted_iota(jnp.int32, (heads, width), 1), 6)
        == lax.broadcasted_iota(jnp.int32, (heads, width), 0)
    ).astype(F32)
    vec[...] = jnp.zeros_like(vec)
    vec[0:1, :] = step_bias[...]
    vec[1:2, :] = decay_log[...]
    vec[2:3, :] = skip_gain[...]
    vec_x[...] = jnp.dot(
        vec[...], spread, precision=lax.Precision.HIGHEST, preferred_element_type=F32
    )
    local[2].wait()
    step_raw = lax.dot_general(
        nrm[...], wt[...], (((1,), (1,)), ((), ())), preferred_element_type=F32
    ).astype(BF16)
    step_x = jnp.dot(step_raw, spread.astype(BF16), preferred_element_type=F32) + vec_x[0:1, :]
    steps[...] = jnp.maximum(step_x, 0.0) + jnp.log1p(jnp.exp(-jnp.abs(step_x)))

    tile = 256
    local[3].wait()

    def project_inner(j, carry):
        cols = pl.ds(pl.multiple_of(j * tile, tile), tile)
        value = jnp.dot(nrm[...], wi[:, cols], preferred_element_type=F32)
        value = value.astype(BF16).astype(F32)
        for r in range(count):
            seq_i[r, 8:16, cols] = value[r * DRAFT : (r + 1) * DRAFT]
        return carry

    lax.fori_loop(0, width // tile, project_inner, 0)
    local[4].wait()

    def project_gate(j, carry):
        cols = pl.ds(pl.multiple_of(j * tile, tile), tile)
        value = jnp.dot(nrm[...], wg[:, cols], preferred_element_type=F32)
        value = value.astype(BF16).astype(F32)
        gate[:, cols] = silu(value)
        return carry

    lax.fori_loop(0, width // tile, project_gate, 0)

    for k in early:
        wires.pass_on(k, relay.at[k], raw.at[early.index(k)])

    ssm_move.wait()
    own_cols = ssm_own[...].astype(F32)
    got_cols = ssm_got[...].astype(F32)
    first = head == 0
    bcols = jnp.where(first, own_cols, got_cols)
    ccols = jnp.where(first, got_cols, own_cols)
    for r in range(count):
        seq_i[r, 5:8, :] = edge_i[r].astype(F32)
        seq_s[r, 5:8, :] = edge_s[r].astype(F32)
        seq_s[r, 8:16, :NSTATE] = bcols[r * DRAFT : (r + 1) * DRAFT]
        seq_s[r, 8:16, NSTATE:] = ccols[r * DRAFT : (r + 1) * DRAFT]

    slot_of = slots

    def one_request(r, carry):
        block = pl.ds(pl.multiple_of(r * DRAFT, DRAFT), DRAFT)
        total = jnp.zeros((DRAFT, width), F32) + lines[1:2, :]
        narrow = jnp.zeros((DRAFT, 2 * NSTATE), F32) + bias_s[...]
        for k in range(KCONV):
            total = total + seq_i[r, 5 + k : 13 + k, :] * conv_i[k : k + 1, :].astype(F32)
            narrow = narrow + seq_s[r, 5 + k : 13 + k, :] * conv_s[k : k + 1, :].astype(F32)
        x = silu(total).astype(BF16).astype(F32)
        bc = silu(narrow).astype(BF16)
        bmat, cmat = bc[:, :NSTATE], bc[:, NSTATE:]
        when = lax.broadcasted_iota(jnp.int32, (DRAFT, width), 0)
        step = jnp.where(when < lengths[r], steps[block, :], 0.0)
        change = step * -jnp.exp(vec_x[1:2, :])
        decay = change
        for shift in (1, 2, 4):
            decay = decay + jnp.where(when >= shift, pltpu.roll(decay, shift, 0), 0.0)
        weighted = step * x
        pair = lax.dot_general(cmat, bmat, (((1,), (1,)), ((), ())), preferred_element_type=F32)
        seen = lax.dot_general(cmat, st[r], (((1,), (1,)), ((), ())), preferred_element_type=F32)
        out = jnp.exp(decay) * seen + vec_x[2:3, :] * x
        for u in range(DRAFT):
            lag = jnp.where(when >= u, decay - decay[u : u + 1, :], -1e30)
            out = out + jnp.exp(lag) * pair[:, u : u + 1] * weighted[u : u + 1, :]
        ssm_out = out.astype(BF16).astype(F32)
        value = ssm_out * gate[block, :]
        gated[block, :] = value
        sq_own[block, :] = jnp.broadcast_to(
            jnp.sum(value * value, axis=-1, keepdims=True), (DRAFT, NSTATE)
        )
        taken = accepted[r]
        end = jnp.sum(jnp.where(when < taken, change, 0.0), axis=0, keepdims=True)
        lag = jnp.where(when < taken, end - decay, -1e30)
        pack_f[r, 0:8, :width] = jnp.exp(lag) * weighted
        whole_decay = jnp.exp(end)
        high = whole_decay.astype(BF16).astype(F32)
        pack_f[r, 8:9, :width] = high
        pack_f[r, 9:10, :width] = whole_decay - high
        pack_f[r, 10:16, :width] = jnp.zeros((6, width), F32)
        pack_f[r, 0:8, width:] = bmat.astype(F32)
        pack_f[r, 8:16, width:] = jnp.zeros((8, NSTATE), F32)
        pack_b[r] = pack_f[r].astype(BF16)
        for i in range(KCONV - 1):
            edge_f[r, i : i + 1, :width] = seq_i[r, pl.ds(5 + taken + i, 1), :]
            edge_f[r, i : i + 1, width:] = seq_s[r, pl.ds(5 + taken + i, 1), :]
        slot = slot_of[0]
        for q in range(1, count):
            slot = jnp.where(r == q, slot_of[q], slot)
        edge_f[r, 3:4, :] = jnp.zeros((1, width + 2 * NSTATE), F32) + slot.astype(F32)
        return carry

    lax.fori_loop(0, count, one_request, 0)

    sq_move = wires.copy(sq_own, sq_got, 2, partner)
    sq_move.start()
    for k in early:
        packs[early.index(k)] = pack_b[picks[k]]
    for k in early:
        wires.go(True, packs.at[early.index(k)], got_pack.at[early.index(k)], 48 + k, wires.at(k))

    def keep(k):
        def state(rows):
            return st[picks[k], rows, :]

        def store(rows, value):
            send[k, rows, :] = value

        spare[...] = pack_b[picks[k]]
        finish_state(state, spare, store)

    for k in late:
        keep(k)
        wires.start_relayed(k, send.at[k], relay.at[k])
        wires.start_direct(k, send.at[k], got_state.at[k])
    for k in range(WINDOW):
        edges[k] = jnp.where(valid[k] > 0, edge_f[picks[k]], -1.0).astype(BF16)
    for k in active:
        wires.go(True, edges.at[k], got_edge.at[k], 56 + k, wires.at(k))
    for k in early:
        wires.pass_round(k, relay.at[k], raw.at[early.index(k)])
    keep(0)
    own_state = pltpu.make_async_copy(send.at[0], got_state.at[0], local_sem.at[6])
    own_state.start()
    own_edges = []
    for k in range(WINDOW):
        if k not in active:
            copy = pltpu.make_async_copy(edges.at[k], got_edge.at[k], local_sem.at[7 + len(own_edges)])
            copy.start()
            own_edges.append(copy)

    sq_move.wait()
    square = (sq_own[:, 0:1] + sq_got[:, 0:1]) / DINNER
    nrm[...] = (gated[...] * lax.rsqrt(square + EPS) * lines[2:3, :]).astype(BF16)

    local[5].wait()
    per = half // tile

    def project_out(j, carry):
        which = jnp.where(j < per, other, head)
        i = jnp.where(j < per, j, j - per)
        cols = pl.ds(pl.multiple_of(which * half + i * tile, tile), tile)
        value = jnp.dot(nrm[...], wo[:, cols], preferred_element_type=F32)
        part[pl.ds(jnp.where(j < per, 0, 1), 1), :, pl.ds(pl.multiple_of(i * tile, tile), tile)] = value[None]
        return carry

    lax.fori_loop(0, per, project_out, 0)
    part_move = wires.copy(part.at[0], part_got, 3, partner)
    part_move.start()
    lax.fori_loop(per, 2 * per, project_out, 0)
    for k in late:
        if k != ROW_LEN:
            wires.pass_on(k, relay.at[k], got_state.at[k])
    for k in late:
        wires.pass_round(k, relay.at[k], got_state.at[k])
    part_move.wait()
    hidden_out[...] = (hid[...].astype(F32) + part[1] + part_got[...]).astype(BF16)

    finals = [own_state] + own_edges
    for k in early:
        i = early.index(k)
        wires.copy(packs.at[i], got_pack.at[i], 48 + k, wires.at(1)).wait_recv()
        wires.arrive(k, raw.at[i])

        def state(rows):
            return raw[i, rows, :]

        def store(rows, value):
            done[i, rows, :] = value

        finish_state(state, got_pack.at[i], store)
        copy = pltpu.make_async_copy(done.at[i], got_state.at[k], local_sem.at[10 + i])
        copy.start()
        finals.append(copy)
    for k in late:
        wires.arrive(k, got_state.at[k])
    for k in active:
        wires.copy(edges.at[k], got_edge.at[k], 56 + k, wires.at(1)).wait_recv()
    wires.drain()
    for copy in finals:
        copy.wait()


def place_kernel(sizes, got_state, got_edge, hidden, kept, kept_i, kept_s, hidden_out, buf, in_sem, out_sem):
    count, width = sizes
    loads = []
    for k in range(WINDOW):
        copy = pltpu.make_async_copy(got_state.at[k], buf.at[k], in_sem.at[k])
        copy.start()
        loads.append(copy)
    hidden_out[...] = hidden[...]
    slots = []
    for k in range(WINDOW):
        slots.append(jnp.max(got_edge[k, 3:4, :128].astype(F32)).astype(jnp.int32))
    for k in range(WINDOW):
        loads[k].wait()

        @pl.when(slots[k] >= 0)
        def _():
            pltpu.make_async_copy(buf.at[k], kept.at[slots[k]], out_sem.at[k]).start()
            kept_i[slots[k]] = got_edge[k, 0:3, :width]
            kept_s[slots[k]] = got_edge[k, 0:3, width:]

    for k in range(WINDOW):

        @pl.when(slots[k] >= 0)
        def _():
            pltpu.make_async_copy(buf.at[k], kept.at[slots[k]], out_sem.at[k]).wait()


def local(
    peers,
    hidden_in,
    norm_gain,
    proj_gate,
    proj_inner,
    proj_ssm,
    proj_step,
    step_bias,
    decay_log,
    skip_gain,
    conv_inner,
    conv_inner_bias,
    conv_ssm,
    conv_ssm_bias,
    gate_gain,
    proj_out,
    states_in,
    edge_inner,
    edge_ssm,
    draft_lengths,
    accepted,
    destination,
):
    count, heads = states_in.shape[0], states_in.shape[1]
    rows, half = hidden_in.shape
    width = proj_gate.shape[1]
    model = proj_gate.shape[0]
    flat = states_in.reshape(count, width, NSTATE)
    pack_width = width + NSTATE
    edge_width = width + 2 * NSTATE
    raws = EARLY
    smem = pl.BlockSpec(memory_space=pltpu.SMEM)
    vmem = pl.BlockSpec(memory_space=pltpu.VMEM)
    hbm = pl.BlockSpec(memory_space=pl.ANY)

    def line(value):
        return value.reshape(1, -1)

    def tiled(value):
        return value.reshape(-1, 128)

    def layer(without, *operands):
        active = tuple(k for k in ORDER if k != without)
        return pl.pallas_call(
            functools.partial(layer_kernel, (peers, count, heads, active)),
            name="layer",
            out_shape=(
                jax.ShapeDtypeStruct((WINDOW, width, NSTATE), BF16),
                jax.ShapeDtypeStruct((WINDOW, 4, edge_width), BF16),
                jax.ShapeDtypeStruct((rows, half), BF16),
            ),
            in_specs=[smem] * 3 + [vmem] * 12 + [hbm] * 6,
            out_specs=(hbm, hbm, vmem),
            scratch_shapes=[
                pltpu.VMEM((model, width), BF16),
                pltpu.VMEM((model, width), BF16),
                pltpu.VMEM((model, NSTATE), BF16),
                pltpu.VMEM((heads, model), BF16),
                pltpu.VMEM((width, model), BF16),
                pltpu.VMEM((count, width, NSTATE), BF16),
                pltpu.VMEM((WINDOW, width, NSTATE), BF16),
                pltpu.VMEM((raws, width, NSTATE), BF16),
                pltpu.VMEM((raws, width, NSTATE), BF16),
                pltpu.VMEM((WINDOW, width, NSTATE), BF16),
                pltpu.VMEM((raws, PACK_ROWS, pack_width), BF16),
                pltpu.VMEM((raws, PACK_ROWS, pack_width), BF16),
                pltpu.VMEM((WINDOW, 4, edge_width), BF16),
                pltpu.VMEM((count, PACK_ROWS, pack_width), F32),
                pltpu.VMEM((count, PACK_ROWS, pack_width), BF16),
                pltpu.VMEM((PACK_ROWS, pack_width), BF16),
                pltpu.VMEM((count, 4, edge_width), F32),
                pltpu.VMEM((8, width), F32),
                pltpu.VMEM((2, rows, half), BF16),
                pltpu.VMEM((rows, model), BF16),
                pltpu.VMEM((count, 16, width), F32),
                pltpu.VMEM((count, 16, 2 * NSTATE), F32),
                pltpu.VMEM((rows, NSTATE), BF16),
                pltpu.VMEM((rows, NSTATE), BF16),
                pltpu.VMEM((rows, width), F32),
                pltpu.VMEM((rows, width), F32),
                pltpu.VMEM((8, heads), F32),
                pltpu.VMEM((8, width), F32),
                pltpu.VMEM((rows, width), F32),
                pltpu.VMEM((rows, NSTATE), F32),
                pltpu.VMEM((rows, NSTATE), F32),
                pltpu.VMEM((2, rows, half), F32),
                pltpu.VMEM((rows, half), F32),
                pltpu.SemaphoreType.DMA((12,)),
                pltpu.SemaphoreType.DMA((144,)),
                pltpu.SemaphoreType.DMA((64,)),
            ],
            compiler_params=pltpu.CompilerParams(
                collective_id=without, has_side_effects=True, vmem_limit_bytes=60 * 1024 * 1024
            ),
        )(*operands)

    operands = (
        draft_lengths,
        accepted,
        destination,
        hidden_in,
        tiled(norm_gain),
        line(step_bias),
        line(decay_log),
        line(skip_gain),
        conv_inner,
        tiled(conv_inner_bias),
        conv_ssm,
        line(conv_ssm_bias),
        tiled(gate_gain),
        edge_inner,
        edge_ssm,
        proj_gate,
        proj_inner,
        proj_ssm,
        proj_step.T,
        proj_out,
        flat,
    )
    reach = (destination // count - lax.axis_index("req")) % peers
    offsets = jnp.arange(WINDOW, dtype=jnp.int32)
    unused = jnp.all(reach[:, None] != offsets[None, :], axis=0)
    larger = jnp.max(jnp.where(unused, offsets, 1))
    got_state, got_edge, hidden_out = lax.switch(
        larger - 1, [functools.partial(layer, k) for k in range(1, WINDOW)], *operands
    )
    kept, kept_i, kept_s, hidden = pl.pallas_call(
        functools.partial(place_kernel, (count, width)),
        name="place",
        out_shape=(
            jax.ShapeDtypeStruct(flat.shape, BF16),
            jax.ShapeDtypeStruct(edge_inner.shape, BF16),
            jax.ShapeDtypeStruct(edge_ssm.shape, BF16),
            jax.ShapeDtypeStruct(hidden_in.shape, BF16),
        ),
        in_specs=[hbm, vmem, vmem],
        out_specs=(hbm, vmem, vmem, vmem),
        scratch_shapes=[
            pltpu.VMEM((WINDOW, width, NSTATE), BF16),
            pltpu.SemaphoreType.DMA((WINDOW,)),
            pltpu.SemaphoreType.DMA((WINDOW,)),
        ],
    )(got_state, got_edge, hidden_out)
    return (hidden, kept.reshape(states_in.shape), kept_i, kept_s)


def solution(mesh):
    in_specs = (
        P("req", "head"),
        P(),
        P(None, "head"),
        P(None, "head"),
        P(None, "head"),
        P(None, "head"),
        P("head"),
        P("head"),
        P("head"),
        P(None, "head"),
        P("head"),
        P(),
        P(),
        P("head"),
        P("head", None),
        P("req", "head", None, None),
        P("req", None, "head"),
        P("req", None, None),
        P("req"),
        P("req"),
        P("req"),
    )
    out_specs = (
        P("req", "head"),
        P("req", "head", None, None),
        P("req", None, "head"),
        P("req", None, None),
    )
    return jax.shard_map(
        functools.partial(local, mesh.shape["req"]),
        mesh=mesh,
        in_specs=in_specs,
        out_specs=out_specs,
        check_vma=False,
    )
```

```python
import functools

import jax
import jax.numpy as jnp
from jax import lax
from jax.experimental import pallas as pl
from jax.experimental.pallas import tpu as pltpu
from jax.sharding import PartitionSpec as P

HEAD_DIM = 64
NSTATE = 128
KCONV = 4
DRAFT = 8
WINDOW = 8
DINNER = 3072
EPS = 1e-05
MESH = pl.DeviceIdType.MESH
F32 = jnp.float32
BF16 = jnp.bfloat16
PACK_ROWS = 16


def silu(value):
    return value * jax.nn.sigmoid(value)


def finish_state(state, factors, store):
    width = factors.shape[1] - NSTATE
    row = lax.broadcasted_iota(jnp.int32, (PACK_ROWS, NSTATE), 0)
    decay = jnp.where((row == 8) | (row == 9), 1.0, 0.0).astype(BF16)
    right = jnp.concatenate([factors[:, pl.ds(width, NSTATE)], decay], axis=1)
    chunk = 512

    def part(i, carry):
        rows = pl.ds(pl.multiple_of(i * chunk, chunk), chunk)
        both = lax.dot_general(
            factors[:, rows], right, (((0,), (0,)), ((), ())), preferred_element_type=F32
        )
        store(rows, (state(rows).astype(F32) * both[:, NSTATE:] + both[:, :NSTATE]).astype(BF16))
        return carry

    lax.fori_loop(0, width // chunk, part, 0)


ORDER = (7, 6, 5, 3, 4, 2, 1)
EARLY = 2
PIECES = {0: ((0, 1536),), 1: ((0, 768), (768, 768)), 2: ((0, 512), (512, 512), (1024, 512))}
OFFSETS = (1, 2, 3, 4, 5, 6, 7, 8, -1, -2, -3, -13, -14, -15, 17, 18, 19, 20, -12)
ROW_LEN, COL_LEN = 4, 8


class Wires:
    def __init__(self, peers, me, head, send_sem, recv_sem):
        self.peers, self.me, self.head = peers, me, head
        self.send_sem, self.recv_sem = send_sem, recv_sem
        self.x = lax.rem(me, ROW_LEN)
        self.y = lax.rem(lax.div(me, ROW_LEN), COL_LEN)
        self.sent = []

    def at(self, offset):
        return {"req": lax.rem(self.me + offset + self.peers, self.peers), "head": self.head}

    def copy(self, src, dst, i, device, out=None):
        return pltpu.make_async_remote_copy(
            src_ref=src,
            dst_ref=dst,
            send_sem=self.send_sem.at[i if out is None else out],
            recv_sem=self.recv_sem.at[i],
            device_id=device,
            device_id_type=MESH,
        )

    def go(self, cond, src, dst, i, device, out=None):
        copy = self.copy(src, dst, i, device, out)
        if cond is True:
            copy.start()
        else:
            pl.when(cond)(copy.start)
        self.sent.append((cond, copy))

    def steps_of(self, k, column):
        cases = sorted({(x + k) // ROW_LEN for x in range(ROW_LEN)})
        steps = lax.div(column + k, ROW_LEN)
        return [(True if len(cases) == 1 else steps == d, d) for d in cases]

    def source_column(self, k):
        return lax.rem(self.x + 2 * ROW_LEN - k, ROW_LEN)

    def up(self, turn):
        if turn > 0:
            return jnp.where(self.y >= 3, -3 * ROW_LEN, (COL_LEN - 3) * ROW_LEN)
        return jnp.where(self.y < COL_LEN - 3, 3 * ROW_LEN, -(COL_LEN - 3) * ROW_LEN)

    def start_relayed(self, k, src, relay):
        if k == ROW_LEN:
            return
        for cond, d in self.steps_of(k, self.x):
            if d == 2:
                rows = pl.ds(*PIECES[d][2])
                self.go(cond, src.at[rows], relay.at[rows], 40 + k, self.at(self.up(1) + k - d * ROW_LEN))
            if d > 0:
                rows = pl.ds(*PIECES[d][1])
                self.go(cond, src.at[rows], relay.at[rows], 24 + k, self.at(k - d * ROW_LEN), 88 + 8 * d + k)

    def start_direct(self, k, src, dst):
        if k == ROW_LEN:
            self.go(True, src, dst, 8 + k, self.at(k))
            return
        for cond, d in self.steps_of(k, self.x):
            rows = pl.ds(*PIECES[d][0])
            self.go(cond, src.at[rows], dst.at[rows], 8 + k, self.at(k), 112 + 8 * d + k)

    def pass_on(self, k, relay, dst):
        for cond, d in self.steps_of(k, self.source_column(k)):
            if d == 0:
                continue
            rows = pl.ds(*PIECES[d][1])

            def wait():
                self.copy(relay.at[rows], relay.at[rows], 24 + k, self.at(1)).wait_recv()

            if cond is True:
                wait()
            else:
                pl.when(cond)(wait)
            self.go(cond, relay.at[rows], dst.at[rows], 16 + k, self.at(d * ROW_LEN), 56 + 8 * d + k)

    def pass_round(self, k, relay, dst):
        for cond, d in self.steps_of(k, self.source_column(k)):
            if d != 2:
                continue
            rows = pl.ds(*PIECES[d][2])

            def wait():
                self.copy(relay.at[rows], relay.at[rows], 40 + k, self.at(1)).wait_recv()

            if cond is True:
                wait()
            else:
                pl.when(cond)(wait)
            self.go(cond, relay.at[rows], dst.at[rows], 32 + k, self.at(self.up(-1) + 2 * ROW_LEN), 80 + k)

    def arrive(self, k, dst):
        if k == ROW_LEN:
            self.copy(dst, dst, 8 + k, self.at(1)).wait_recv()
            return
        for cond, d in self.steps_of(k, self.source_column(k)):

            def wait():
                for i, piece in enumerate(PIECES[d]):
                    rows = pl.ds(*piece)
                    self.copy(dst.at[rows], dst.at[rows], 8 + 8 * i + k if i < 2 else 32 + k, self.at(1)).wait_recv()

            if cond is True:
                wait()
            else:
                pl.when(cond)(wait)

    def drain(self):
        for cond, copy in self.sent:
            if cond is True:
                copy.wait_send()
            else:
                pl.when(cond)(copy.wait_send)


def layer_kernel(
    sizes,
    lengths,
    accepted,
    destination,
    hid,
    norm_gain,
    step_bias,
    decay_log,
    skip_gain,
    conv_i,
    bias_i,
    conv_s,
    bias_s,
    gate_gain,
    edge_i,
    edge_s,
    wg_hbm,
    wi_hbm,
    ws_hbm,
    wt_hbm,
    wo_hbm,
    st_hbm,
    got_state,
    got_edge,
    hidden_out,
    wg,
    wi,
    ws,
    wt,
    wo,
    st,
    send,
    raw,
    done,
    relay,
    packs,
    got_pack,
    edges,
    pack_f,
    pack_b,
    spare,
    edge_f,
    lines,
    whole,
    nrm,
    seq_i,
    seq_s,
    ssm_own,
    ssm_got,
    gate,
    steps,
    inner,
    fed,
    mixed,
    vec,
    vec_x,
    gated,
    sq_own,
    sq_got,
    part,
    part_got,
    local_sem,
    send_sem,
    recv_sem,
):
    peers, count, heads, active = sizes
    early, late = active[:EARLY], active[EARLY:]
    rows = count * DRAFT
    half = hid.shape[1]
    width = wg.shape[1]
    me = lax.axis_index("req")
    head = lax.axis_index("head")
    other = 1 - head

    local = []
    for i, (src, dst) in enumerate(
        (
            (st_hbm, st),
            (ws_hbm, ws),
            (wt_hbm, wt),
            (wi_hbm, wi),
            (wg_hbm, wg),
            (wo_hbm, wo),
        )
    ):
        local.append(pltpu.make_async_copy(src, dst, local_sem.at[i]))
    for copy in local[:4]:
        copy.start()

    wires = Wires(peers, me, head, send_sem, recv_sem)
    partner = {"req": me, "head": other}
    barrier = pltpu.get_barrier_semaphore()
    for offset in OFFSETS:
        pl.semaphore_signal(barrier, inc=1, device_id=wires.at(-offset), device_id_type=MESH)
    pl.semaphore_signal(barrier, inc=1, device_id=partner, device_id_type=MESH)
    pl.semaphore_wait(barrier, len(OFFSETS) + 1)
    for copy in local[4:]:
        copy.start()

    to_partner = wires.copy(hid, whole.at[head], 0, partner)
    to_partner.start()

    reach, slots = [], []
    for r in range(count):
        target = destination[r]
        owner = lax.div(target, count)
        reach.append(lax.rem(owner - me + peers, peers))
        slots.append(target - owner * count)
    picks, valid = [], []
    for k in range(WINDOW):
        pick = jnp.int32(0)
        found = jnp.int32(0)
        for r in range(count):
            hit = reach[r] == k
            pick = jnp.where(hit, jnp.int32(r), pick)
            found = jnp.where(hit, jnp.int32(1), found)
        picks.append(pick)
        valid.append(found)

    local[0].wait()
    for k in early:
        send[k] = st[picks[k]]
    for k in early:
        wires.start_relayed(k, send.at[k], relay.at[k])
    for k in early:
        wires.start_direct(k, send.at[k], raw.at[early.index(k)])

    for i in range(width // 128):
        cols = slice(i * 128, (i + 1) * 128)
        lines[0:1, cols] = norm_gain[i : i + 1, :]
        lines[1:2, cols] = bias_i[i : i + 1, :]
        lines[2:3, cols] = gate_gain[i : i + 1, :]
    whole[pl.ds(head, 1)] = hid[...][None]
    to_partner.wait()
    left = whole[0].astype(F32)
    right = whole[1].astype(F32)
    mean = (
        jnp.sum(left * left, axis=-1, keepdims=True) + jnp.sum(right * right, axis=-1, keepdims=True)
    ) / (2 * half)
    scale = lax.rsqrt(mean + EPS)
    nrm[:, :half] = (left * scale * lines[0:1, :half]).astype(BF16)
    nrm[:, half:] = (right * scale * lines[0:1, half:]).astype(BF16)

    local[1].wait()
    ssm_own[...] = jnp.dot(nrm[...], ws[...], preferred_element_type=F32).astype(BF16)
    ssm_move = wires.copy(ssm_own, ssm_got, 1, partner)
    ssm_move.start()

    spread = (
        lax.shift_right_logical(lax.broadcasted_iota(jnp.int32, (heads, width), 1), 6)
        == lax.broadcasted_iota(jnp.int32, (heads, width), 0)
    ).astype(F32)
    vec[...] = jnp.zeros_like(vec)
    vec[0:1, :] = step_bias[...]
    vec[1:2, :] = decay_log[...]
    vec[2:3, :] = skip_gain[...]
    vec_x[...] = jnp.dot(
        vec[...], spread, precision=lax.Precision.HIGHEST, preferred_element_type=F32
    )
    local[2].wait()
    step_raw = lax.dot_general(
        nrm[...], wt[...], (((1,), (1,)), ((), ())), preferred_element_type=F32
    ).astype(BF16)
    step_x = jnp.dot(step_raw, spread.astype(BF16), preferred_element_type=F32) + vec_x[0:1, :]
    steps[...] = jnp.maximum(step_x, 0.0) + jnp.log1p(jnp.exp(-jnp.abs(step_x)))

    tile = 256
    local[3].wait()

    def project_inner(j, carry):
        cols = pl.ds(pl.multiple_of(j * tile, tile), tile)
        value = jnp.dot(nrm[...], wi[:, cols], preferred_element_type=F32)
        value = value.astype(BF16).astype(F32)
        for r in range(count):
            seq_i[r, 8:16, cols] = value[r * DRAFT : (r + 1) * DRAFT]
        return carry

    lax.fori_loop(0, width // tile, project_inner, 0)
    ssm_move.wait()
    own_cols = ssm_own[...].astype(F32)
    got_cols = ssm_got[...].astype(F32)
    first = head == 0
    bcols = jnp.where(first, own_cols, got_cols)
    ccols = jnp.where(first, got_cols, own_cols)
    for r in range(count):
        seq_i[r, 5:8, :] = edge_i[r].astype(F32)
        seq_s[r, 5:8, :] = edge_s[r].astype(F32)
        seq_s[r, 8:16, :NSTATE] = bcols[r * DRAFT : (r + 1) * DRAFT]
        seq_s[r, 8:16, NSTATE:] = ccols[r * DRAFT : (r + 1) * DRAFT]

    slot_of = slots

    def one_request(r, carry):
        block = pl.ds(pl.multiple_of(r * DRAFT, DRAFT), DRAFT)
        total = jnp.zeros((DRAFT, width), F32) + lines[1:2, :]
        narrow = jnp.zeros((DRAFT, 2 * NSTATE), F32) + bias_s[...]
        for k in range(KCONV):
            total = total + seq_i[r, 5 + k : 13 + k, :] * conv_i[k : k + 1, :].astype(F32)
            narrow = narrow + seq_s[r, 5 + k : 13 + k, :] * conv_s[k : k + 1, :].astype(F32)
        x = silu(total).astype(BF16).astype(F32)
        bc = silu(narrow).astype(BF16)
        bmat = bc[:, :NSTATE]
        when = lax.broadcasted_iota(jnp.int32, (DRAFT, width), 0)
        step = jnp.where(when < lengths[r], steps[block, :], 0.0)
        change = step * -jnp.exp(vec_x[1:2, :])
        decay = change
        for shift in (1, 2, 4):
            decay = decay + jnp.where(when >= shift, pltpu.roll(decay, shift, 0), 0.0)
        weighted = step * x
        mixed[r] = bc.astype(F32)
        inner[block, :] = x
        steps[block, :] = decay
        fed[block, :] = weighted
        taken = accepted[r]
        end = jnp.sum(jnp.where(when < taken, change, 0.0), axis=0, keepdims=True)
        lag = jnp.where(when < taken, end - decay, -1e30)
        pack_f[r, 0:8, :width] = jnp.exp(lag) * weighted
        whole_decay = jnp.exp(end)
        high = whole_decay.astype(BF16).astype(F32)
        pack_f[r, 8:9, :width] = high
        pack_f[r, 9:10, :width] = whole_decay - high
        pack_f[r, 10:16, :width] = jnp.zeros((6, width), F32)
        pack_f[r, 0:8, width:] = bmat.astype(F32)
        pack_f[r, 8:16, width:] = jnp.zeros((8, NSTATE), F32)
        pack_b[r] = pack_f[r].astype(BF16)
        for i in range(KCONV - 1):
            edge_f[r, i : i + 1, :width] = seq_i[r, pl.ds(5 + taken + i, 1), :]
            edge_f[r, i : i + 1, width:] = seq_s[r, pl.ds(5 + taken + i, 1), :]
        slot = slot_of[0]
        for q in range(1, count):
            slot = jnp.where(r == q, slot_of[q], slot)
        edge_f[r, 3:4, :] = jnp.zeros((1, width + 2 * NSTATE), F32) + slot.astype(F32)
        return carry

    lax.fori_loop(0, count, one_request, 0)

    for k in early:
        packs[early.index(k)] = pack_b[picks[k]]
    for k in early:
        wires.go(True, packs.at[early.index(k)], got_pack.at[early.index(k)], 48 + k, wires.at(k))

    def keep(k):
        def state(rows):
            return st[picks[k], rows, :]

        def store(rows, value):
            send[k, rows, :] = value

        spare[...] = pack_b[picks[k]]
        finish_state(state, spare, store)

    for k in late:
        keep(k)
        wires.start_relayed(k, send.at[k], relay.at[k])
        wires.start_direct(k, send.at[k], got_state.at[k])
    for k in range(WINDOW):
        edges[k] = jnp.where(valid[k] > 0, edge_f[picks[k]], -1.0).astype(BF16)
    for k in active:
        wires.go(True, edges.at[k], got_edge.at[k], 56 + k, wires.at(k))
    for k in early:
        wires.pass_on(k, relay.at[k], raw.at[early.index(k)])

    local[4].wait()

    def project_gate(j, carry):
        cols = pl.ds(pl.multiple_of(j * tile, tile), tile)
        value = jnp.dot(nrm[...], wg[:, cols], preferred_element_type=F32)
        value = value.astype(BF16).astype(F32)
        gate[:, cols] = silu(value)
        return carry

    lax.fori_loop(0, width // tile, project_gate, 0)

    for k in early:
        wires.pass_round(k, relay.at[k], raw.at[early.index(k)])
    keep(0)
    own_state = pltpu.make_async_copy(send.at[0], got_state.at[0], local_sem.at[6])
    own_state.start()
    own_edges = []
    for k in range(WINDOW):
        if k not in active:
            copy = pltpu.make_async_copy(edges.at[k], got_edge.at[k], local_sem.at[7 + len(own_edges)])
            copy.start()
            own_edges.append(copy)

    def one_output(r, carry):
        block = pl.ds(pl.multiple_of(r * DRAFT, DRAFT), DRAFT)
        bc = mixed[r].astype(BF16)
        bmat, cmat = bc[:, :NSTATE], bc[:, NSTATE:]
        x = inner[block, :]
        decay = steps[block, :]
        weighted = fed[block, :]
        when = lax.broadcasted_iota(jnp.int32, (DRAFT, width), 0)
        pair = lax.dot_general(cmat, bmat, (((1,), (1,)), ((), ())), preferred_element_type=F32)
        seen = lax.dot_general(cmat, st[r], (((1,), (1,)), ((), ())), preferred_element_type=F32)
        out = jnp.exp(decay) * seen + vec_x[2:3, :] * x
        for u in range(DRAFT):
            lag = jnp.where(when >= u, decay - decay[u : u + 1, :], -1e30)
            out = out + jnp.exp(lag) * pair[:, u : u + 1] * weighted[u : u + 1, :]
        ssm_out = out.astype(BF16).astype(F32)
        value = ssm_out * gate[block, :]
        gated[block, :] = value
        sq_own[block, :] = jnp.broadcast_to(
            jnp.sum(value * value, axis=-1, keepdims=True), (DRAFT, NSTATE)
        )
        return carry

    lax.fori_loop(0, count, one_output, 0)
    sq_move = wires.copy(sq_own, sq_got, 2, partner)
    sq_move.start()

    for k in late:
        if k != ROW_LEN:
            wires.pass_on(k, relay.at[k], got_state.at[k])
    sq_move.wait()
    square = (sq_own[:, 0:1] + sq_got[:, 0:1]) / DINNER
    nrm[...] = (gated[...] * lax.rsqrt(square + EPS) * lines[2:3, :]).astype(BF16)

    local[5].wait()
    per = half // tile

    def project_out(j, carry):
        which = jnp.where(j < per, other, head)
        i = jnp.where(j < per, j, j - per)
        cols = pl.ds(pl.multiple_of(which * half + i * tile, tile), tile)
        value = jnp.dot(nrm[...], wo[:, cols], preferred_element_type=F32)
        part[pl.ds(jnp.where(j < per, 0, 1), 1), :, pl.ds(pl.multiple_of(i * tile, tile), tile)] = value[None]
        return carry

    lax.fori_loop(0, per, project_out, 0)
    part_move = wires.copy(part.at[0], part_got, 3, partner)
    part_move.start()
    lax.fori_loop(per, 2 * per, project_out, 0)
    for k in late:
        wires.pass_round(k, relay.at[k], got_state.at[k])
    part_move.wait()
    hidden_out[...] = (hid[...].astype(F32) + part[1] + part_got[...]).astype(BF16)

    finals = [own_state] + own_edges
    for k in early:
        i = early.index(k)
        wires.copy(packs.at[i], got_pack.at[i], 48 + k, wires.at(1)).wait_recv()
        wires.arrive(k, raw.at[i])

        def state(rows):
            return raw[i, rows, :]

        def store(rows, value):
            done[i, rows, :] = value

        finish_state(state, got_pack.at[i], store)
        copy = pltpu.make_async_copy(done.at[i], got_state.at[k], local_sem.at[10 + i])
        copy.start()
        finals.append(copy)
    for k in late:
        wires.arrive(k, got_state.at[k])
    for k in active:
        wires.copy(edges.at[k], got_edge.at[k], 56 + k, wires.at(1)).wait_recv()
    wires.drain()
    for copy in finals:
        copy.wait()


def place_kernel(
    sizes, got_state, got_edge, hidden, kept, kept_i, kept_s, hidden_out, edge, hid, edge_i, edge_s, in_sem, out_sem
):
    count, width = sizes
    edge_in = pltpu.make_async_copy(got_edge, edge, in_sem.at[0])
    edge_in.start()
    hid_in = pltpu.make_async_copy(hidden, hid, in_sem.at[1])
    hid_in.start()
    edge_in.wait()
    slots = []
    for k in range(WINDOW):
        slots.append(jnp.max(edge[k, 3:4, :128].astype(F32)).astype(jnp.int32))
    for k in range(WINDOW):

        @pl.when(slots[k] >= 0)
        def _():
            pltpu.make_async_copy(got_state.at[k], kept.at[slots[k]], out_sem.at[k]).start()

    for k in range(WINDOW):

        @pl.when(slots[k] >= 0)
        def _():
            edge_i[slots[k]] = edge[k, 0:3, :width]
            edge_s[slots[k]] = edge[k, 0:3, width:]

    hid_in.wait()
    outs = []
    for i, (src, dst) in enumerate(((hid, hidden_out), (edge_i, kept_i), (edge_s, kept_s))):
        copy = pltpu.make_async_copy(src, dst, out_sem.at[WINDOW + i])
        copy.start()
        outs.append(copy)
    for k in range(WINDOW):

        @pl.when(slots[k] >= 0)
        def _():
            pltpu.make_async_copy(got_state.at[k], kept.at[slots[k]], out_sem.at[k]).wait()

    for copy in outs:
        copy.wait()


def local(
    peers,
    hidden_in,
    norm_gain,
    proj_gate,
    proj_inner,
    proj_ssm,
    proj_step,
    step_bias,
    decay_log,
    skip_gain,
    conv_inner,
    conv_inner_bias,
    conv_ssm,
    conv_ssm_bias,
    gate_gain,
    proj_out,
    states_in,
    edge_inner,
    edge_ssm,
    draft_lengths,
    accepted,
    destination,
):
    count, heads = states_in.shape[0], states_in.shape[1]
    rows, half = hidden_in.shape
    width = proj_gate.shape[1]
    model = proj_gate.shape[0]
    flat = states_in.reshape(count, width, NSTATE)
    pack_width = width + NSTATE
    edge_width = width + 2 * NSTATE
    raws = EARLY
    smem = pl.BlockSpec(memory_space=pltpu.SMEM)
    vmem = pl.BlockSpec(memory_space=pltpu.VMEM)
    hbm = pl.BlockSpec(memory_space=pl.ANY)

    def line(value):
        return value.reshape(1, -1)

    def tiled(value):
        return value.reshape(-1, 128)

    def layer(without, *operands):
        active = tuple(k for k in ORDER if k != without)
        return pl.pallas_call(
            functools.partial(layer_kernel, (peers, count, heads, active)),
            name="layer",
            out_shape=(
                jax.ShapeDtypeStruct((WINDOW, width, NSTATE), BF16),
                jax.ShapeDtypeStruct((WINDOW, 4, edge_width), BF16),
                jax.ShapeDtypeStruct((rows, half), BF16),
            ),
            in_specs=[smem] * 3 + [vmem] * 12 + [hbm] * 6,
            out_specs=(hbm, hbm, vmem),
            scratch_shapes=[
                pltpu.VMEM((model, width), BF16),
                pltpu.VMEM((model, width), BF16),
                pltpu.VMEM((model, NSTATE), BF16),
                pltpu.VMEM((heads, model), BF16),
                pltpu.VMEM((width, model), BF16),
                pltpu.VMEM((count, width, NSTATE), BF16),
                pltpu.VMEM((WINDOW, width, NSTATE), BF16),
                pltpu.VMEM((raws, width, NSTATE), BF16),
                pltpu.VMEM((raws, width, NSTATE), BF16),
                pltpu.VMEM((WINDOW, width, NSTATE), BF16),
                pltpu.VMEM((raws, PACK_ROWS, pack_width), BF16),
                pltpu.VMEM((raws, PACK_ROWS, pack_width), BF16),
                pltpu.VMEM((WINDOW, 4, edge_width), BF16),
                pltpu.VMEM((count, PACK_ROWS, pack_width), F32),
                pltpu.VMEM((count, PACK_ROWS, pack_width), BF16),
                pltpu.VMEM((PACK_ROWS, pack_width), BF16),
                pltpu.VMEM((count, 4, edge_width), F32),
                pltpu.VMEM((8, width), F32),
                pltpu.VMEM((2, rows, half), BF16),
                pltpu.VMEM((rows, model), BF16),
                pltpu.VMEM((count, 16, width), F32),
                pltpu.VMEM((count, 16, 2 * NSTATE), F32),
                pltpu.VMEM((rows, NSTATE), BF16),
                pltpu.VMEM((rows, NSTATE), BF16),
                pltpu.VMEM((rows, width), F32),
                pltpu.VMEM((rows, width), F32),
                pltpu.VMEM((rows, width), F32),
                pltpu.VMEM((rows, width), F32),
                pltpu.VMEM((count, DRAFT, 2 * NSTATE), F32),
                pltpu.VMEM((8, heads), F32),
                pltpu.VMEM((8, width), F32),
                pltpu.VMEM((rows, width), F32),
                pltpu.VMEM((rows, NSTATE), F32),
                pltpu.VMEM((rows, NSTATE), F32),
                pltpu.VMEM((2, rows, half), F32),
                pltpu.VMEM((rows, half), F32),
                pltpu.SemaphoreType.DMA((12,)),
                pltpu.SemaphoreType.DMA((144,)),
                pltpu.SemaphoreType.DMA((64,)),
            ],
            compiler_params=pltpu.CompilerParams(
                collective_id=without, has_side_effects=True, vmem_limit_bytes=60 * 1024 * 1024
            ),
        )(*operands)

    operands = (
        draft_lengths,
        accepted,
        destination,
        hidden_in,
        tiled(norm_gain),
        line(step_bias),
        line(decay_log),
        line(skip_gain),
        conv_inner,
        tiled(conv_inner_bias),
        conv_ssm,
        line(conv_ssm_bias),
        tiled(gate_gain),
        edge_inner,
        edge_ssm,
        proj_gate,
        proj_inner,
        proj_ssm,
        proj_step.T,
        proj_out,
        flat,
    )
    reach = (destination // count - lax.axis_index("req")) % peers
    offsets = jnp.arange(WINDOW, dtype=jnp.int32)
    unused = jnp.all(reach[:, None] != offsets[None, :], axis=0)
    larger = jnp.max(jnp.where(unused, offsets, 1))
    got_state, got_edge, hidden_out = lax.switch(
        larger - 1, [functools.partial(layer, k) for k in range(1, WINDOW)], *operands
    )
    kept, kept_i, kept_s, hidden = pl.pallas_call(
        functools.partial(place_kernel, (count, width)),
        name="place",
        out_shape=(
            jax.ShapeDtypeStruct(flat.shape, BF16),
            jax.ShapeDtypeStruct(edge_inner.shape, BF16),
            jax.ShapeDtypeStruct(edge_ssm.shape, BF16),
            jax.ShapeDtypeStruct(hidden_in.shape, BF16),
        ),
        in_specs=[hbm, hbm, hbm],
        out_specs=(hbm, hbm, hbm, hbm),
        scratch_shapes=[
            pltpu.VMEM((WINDOW, 4, edge_width), BF16),
            pltpu.VMEM(hidden_in.shape, BF16),
            pltpu.VMEM(edge_inner.shape, BF16),
            pltpu.VMEM(edge_ssm.shape, BF16),
            pltpu.SemaphoreType.DMA((2,)),
            pltpu.SemaphoreType.DMA((WINDOW + 3,)),
        ],
        compiler_params=pltpu.CompilerParams(vmem_limit_bytes=32 * 1024 * 1024),
    )(got_state, got_edge, hidden_out)
    return (hidden, kept.reshape(states_in.shape), kept_i, kept_s)


def solution(mesh):
    in_specs = (
        P("req", "head"),
        P(),
        P(None, "head"),
        P(None, "head"),
        P(None, "head"),
        P(None, "head"),
        P("head"),
        P("head"),
        P("head"),
        P(None, "head"),
        P("head"),
        P(),
        P(),
        P("head"),
        P("head", None),
        P("req", "head", None, None),
        P("req", None, "head"),
        P("req", None, None),
        P("req"),
        P("req"),
        P("req"),
    )
    out_specs = (
        P("req", "head"),
        P("req", "head", None, None),
        P("req", None, "head"),
        P("req", None, None),
    )
    return jax.shard_map(
        functools.partial(local, mesh.shape["req"]),
        mesh=mesh,
        in_specs=in_specs,
        out_specs=out_specs,
        check_vma=False,
    )
```
